32 devices in a mesh: grp: 2 (over y), train: 4 (over z), test: 2 (over x), proj: 2 (over core).
Axes of the slice: x: 2, y: 2, z: 4, core: 2. Of those that a mesh axis runs over, the one named last changes fastest.
Arguments:
- train_windows: bfloat16 [1024, 64, 512], P(('grp', 'test', 'train')), parts along dimension 0, may hold values from -6 to 6
- test_windows: bfloat16 [256, 64, 512], P(('grp', 'train', 'test')), parts along dimension 0, may hold values from -6 to 6
- train_labels: int32 [1024], P(('grp', 'test', 'train')), parts along dimension 0, may hold values from 0 to 7
- test_labels: int32 [256], P(('grp', 'train', 'test')), parts along dimension 0, may hold values from 0 to 7
- dilated_weight: bfloat16 [3, 512, 512], P(None, None, 'proj'), may hold values from -0.15625 to 0.15625
- branch_gain: float32 [512], P('proj'), may hold values from 0.25 to 1.75
- cls_weight: float32 [512, 8], P('proj'), may hold values from -0.75 to 0.75
- sign_seeds: int32 [4096], P('proj'), may hold values from 0 to 1073741823
- precond: float32 [2048], replicated, may hold values from 0.25 to 4
Outputs:
- scores: float32 [256, 512], P(('grp', 'train'), ('test', 'proj')), parts along dimension 0
The draws below stay inside these ranges and needn't reach their ends.
There are 2 independent parts, one for each index of `grp`. The reference program is written for one: setup_inputs(seed, part) draws one part's arguments, and reference() takes and returns one part's arrays. A program takes and returns all parts, laid end to end along the dimension named above; an argument that names none is the same for every part. Nothing has to cross between parts.
All inputs are finite; a program needn't handle non-finite values.
Results may differ from the reference program's by a relative error of at most 0.00038.
Values may be sent and summed in bfloat16 or wider, within the bound.
No kernel may reach another device: no remote copies, remote signals or barrier semaphores. Data moves between devices by JAX's collectives and lax.ppermute only.
A program may use at most 64 MiB of HBM per device.

```python
import math
import jax
import jax.numpy as jnp
from jax import lax

C = 512
NCLS = 8
K = 2048
WINDOW_LENGTH = 64
DILATION_STEP = 4
NTRAIN = 512
NTEST = 128


def with_ends(values, key, least, high):
    dims = values.shape
    place = [jax.random.randint(jax.random.fold_in(key, axis), (), 0, dims[axis]) for axis in range(len(dims))]
    values = values.at[tuple(place)].set(least)
    longest = dims.index(max(dims))
    place[longest] = (place[longest] + 1) % dims[longest]
    return values.at[tuple(place)].set(high)


def steps_of(own_key, extent, split, smallest, high):
    level = 1.0
    for position, shards_of in split:
        steps = jax.random.uniform(jax.random.fold_in(jax.random.fold_in(own_key, 6), position), (shards_of,), jnp.float32, smallest / len(split), high / len(split))
        level = level * jnp.repeat(jnp.exp(steps), extent[position] // shards_of).reshape((-1,) + (1,) * (len(extent) - 1 - position))
    return level


def bell_draw(own_key, extent, deviation, bound, cuts=(), held_as=jnp.bfloat16):
    drawn = jax.random.normal(own_key, extent, jnp.float32) * deviation
    if len(cuts) > 0:
        drawn = steps_of(own_key, extent, cuts, -0.22, 0.18) * drawn
    return jnp.clip(drawn, min=-bound, max=bound).astype(held_as)


def setup_inputs(seed: int = 0, part: int = 0) -> dict:
    key_list = jax.random.split(jax.random.key(seed), 10)
    part_keys = jax.random.split(jax.random.fold_in(key_list[9], part), 10)
    return {
        "train_windows": bell_draw(part_keys[0], (NTRAIN, WINDOW_LENGTH, C), 1.0, 6.0, ((0, 8),)),
        "test_windows": bell_draw(part_keys[1], (NTEST, WINDOW_LENGTH, C), 1.0, 6.0, ((0, 8),)),
        "train_labels": with_ends(jax.random.randint(part_keys[2], (NTRAIN,), 0, NCLS), jax.random.fold_in(part_keys[2], 1), 0, NCLS - 1).astype(jnp.int32),
        "test_labels": with_ends(jax.random.randint(part_keys[3], (NTEST,), 0, NCLS), jax.random.fold_in(part_keys[3], 1), 0, NCLS - 1).astype(jnp.int32),
        "dilated_weight": bell_draw(key_list[4], (3, C, C), (3 * C) ** -0.5, 0.15625, ((2, 2),)),
        "branch_gain": jnp.clip(1.0 + 0.15 * jax.random.normal(key_list[5], (C,), jnp.float32), 0.25, 1.75),
        "cls_weight": bell_draw(key_list[6], (C, NCLS), (C // 8) ** -0.5, 0.75, ((0, 2),), jnp.float32),
        "sign_seeds": with_ends(jax.random.randint(key_list[7], (C * NCLS,), 0, 2 ** 30), jax.random.fold_in(key_list[7], 1), 0, (2 ** 30) - 1).astype(jnp.int32),
        "precond": jnp.clip(jnp.exp(jax.random.uniform(key_list[8], (K,), jnp.float32, math.log(0.25), math.log(4.0))), 0.25, 4.0),
    }


def sign_block(seed_rows, first_col, count):
    columns = jnp.arange(count, dtype=jnp.int32) + first_col
    mixed = seed_rows[:, None] ^ columns[None, :] * 668265261
    mixed = mixed * 625341585
    mixed = mixed ^ mixed >> 13
    mixed = mixed * 1274126177
    picked = mixed >> 16 & 1
    return (1 - 2 * picked).astype(jnp.bfloat16)

def features(window_batch, labels, dilated_weight, branch_gain, cls_weight, signs):
    rows = window_batch.shape[0]
    step_rows = min(rows, 64)
    grouped = window_batch.reshape(rows // step_rows, step_rows, WINDOW_LENGTH, C)
    grouped_labels = labels.reshape(rows // step_rows, step_rows)

    def one_block(inputs):
        windows_at_block, block_labels = inputs
        zero_padded_input = jnp.pad(windows_at_block, ((0, 0), (DILATION_STEP, DILATION_STEP), (0, 0))).astype(jnp.float32)
        convolved_output = jnp.zeros((step_rows, WINDOW_LENGTH, C), jnp.float32)
        for filter_tap_index in range(3):
            convolved_output = convolved_output + jnp.einsum('rua,al->rul', zero_padded_input[:, filter_tap_index * DILATION_STEP:filter_tap_index * DILATION_STEP + WINDOW_LENGTH], dilated_weight[filter_tap_index].astype(jnp.float32), precision=lax.Precision.HIGHEST)
        pooled = lax.optimization_barrier(jnp.mean(windows_at_block.astype(jnp.float32) + branch_gain * jax.nn.relu(convolved_output), axis=1))
        logits = jnp.dot(pooled, cls_weight, precision=lax.Precision.HIGHEST)
        chance = 1.0 / (1.0 + jnp.exp(-logits))
        target = (jnp.arange(NCLS, dtype=jnp.int32)[None, :] == block_labels[:, None]).astype(jnp.float32)
        residue = chance - target
        retain_weight = 1.0 - lax.optimization_barrier(jnp.sum(chance * target, axis=1))
        gradient = (pooled[:, :, None] * residue[:, None, :]).reshape(step_rows, C * NCLS).astype(jnp.bfloat16)
        return (jnp.dot(gradient, signs, preferred_element_type=jnp.float32), retain_weight)
    projected, retained = lax.map(one_block, (grouped, grouped_labels))
    return (projected.reshape(rows, K), retained.reshape(rows))

def reference(train_windows, test_windows, train_labels, test_labels, dilated_weight, branch_gain, cls_weight, sign_seeds, precond):
    signs = sign_block(sign_seeds, 0, K)
    train_proj, train_retain = features(train_windows, train_labels, dilated_weight, branch_gain, cls_weight, signs)
    test_proj, test_retain = features(test_windows, test_labels, dilated_weight, branch_gain, cls_weight, signs)
    train_feat = (train_proj * train_retain[:, None]).astype(jnp.bfloat16)
    test_feat = (test_proj * precond[None, :]).astype(jnp.bfloat16)
    score_scale = 1.0 / (K * math.sqrt(C))
    return jnp.dot(test_feat, train_feat.T, preferred_element_type=jnp.float32) * score_scale
```

```python
import functools
import math

import jax
import jax.numpy as jnp
from jax import lax
from jax.experimental import pallas as pl
from jax.experimental.pallas import tpu as pltpu
from jax.sharding import PartitionSpec as P

C = 512
NCLS = 8
K = 2048
DILATION_STEP = 4
MIX_COLUMN = 668265261
MIX_FIRST = 625341585
MIX_LAST = (1274126177 << 15) & 0xFFFFFFFF
MIX_LAST = MIX_LAST - (1 << 32) if MIX_LAST >= 1 << 31 else MIX_LAST
MIB = 2**20

VMEM = pl.BlockSpec(memory_space=pltpu.VMEM)
HBM = pl.BlockSpec(memory_space=pltpu.HBM)


def pool_kernel(
    block,
    train_hbm,
    test_hbm,
    weight_hbm,
    gain_ref,
    cls_ref,
    train_label_ref,
    test_label_ref,
    train_packet,
    test_packet,
    rows,
    weight,
    pooled,
    row_sem,
    weight_sem,
):
    proj_index = lax.axis_index("proj")
    train_count, length, width = train_hbm.shape
    test_count = test_hbm.shape[0]
    half = weight.shape[2]
    blocks = (train_count + test_count) // block
    weight_copy = pltpu.make_async_copy(weight_hbm, weight, weight_sem)
    weight_copy.start()
    for b in range(blocks):
        source = train_hbm if b < train_count // block else test_hbm
        offset = b * block if b < train_count // block else b * block - train_count
        pltpu.make_async_copy(
            source.at[pl.ds(offset, block)], rows.at[pl.ds(b * block, block)], row_sem.at[b]
        ).start()
    weight_copy.wait()
    gain = gain_ref[...]
    own_start = pl.multiple_of(proj_index * half, half)

    def one_block(b, carry):
        start = b * block
        pltpu.make_async_copy(
            test_hbm.at[pl.ds(0, block)], rows.at[pl.ds(start, block)], row_sem.at[b]
        ).wait()
        x = rows[pl.ds(start, block)]
        zeros = jnp.zeros((block, DILATION_STEP, width), x.dtype)
        before = jnp.concatenate([zeros, x[:, : length - DILATION_STEP]], axis=1)
        after = jnp.concatenate([x[:, DILATION_STEP:], zeros], axis=1)
        taps = jnp.concatenate([before, x, after], axis=2).reshape(block * length, 3 * width)
        conv = jnp.dot(
            taps, weight[...].reshape(3 * width, half), preferred_element_type=jnp.float32
        ).reshape(block, length, half)
        own = rows[pl.ds(start, block), :, pl.ds(own_start, half)].astype(jnp.float32)
        total = jnp.sum(own, axis=1) + gain * jnp.sum(jnp.maximum(conv, 0.0), axis=1)
        pooled[pl.ds(pl.multiple_of(start, block), block), :] = total * (1.0 / length)
        return carry

    lax.fori_loop(0, blocks, one_block, 0)
    for packet, label_ref, start, count in (
        (train_packet, train_label_ref, 0, train_count),
        (test_packet, test_label_ref, train_count, test_count),
    ):
        own = pooled[pl.ds(start, count), :]
        packet[pl.ds(0, count), :] = own
        packet[pl.ds(count, NCLS), pl.ds(0, count)] = lax.dot_general(
            cls_ref[...],
            own,
            (((1,), (1,)), ((), ())),
            precision=lax.Precision.HIGHEST,
            preferred_element_type=jnp.float32,
        )
        packet[pl.ds(count, NCLS), pl.ds(128, count)] = jnp.broadcast_to(
            label_ref[...].astype(jnp.float32), (NCLS, count)
        )


def pool(train_windows, test_windows, weight, gain, cls_t, train_labels, test_labels):
    block = 8
    train_count, length, width = train_windows.shape
    test_count = test_windows.shape[0]
    half = weight.shape[2]
    total = train_count + test_count
    return pl.pallas_call(
        functools.partial(pool_kernel, block),
        out_shape=(
            jax.ShapeDtypeStruct((train_count + NCLS, half), jnp.float32),
            jax.ShapeDtypeStruct((test_count + NCLS, half), jnp.float32),
        ),
        in_specs=[HBM, HBM, HBM, VMEM, VMEM, VMEM, VMEM],
        out_specs=(VMEM, VMEM),
        scratch_shapes=[
            pltpu.VMEM((total, length, width), jnp.bfloat16),
            pltpu.VMEM(weight.shape, jnp.bfloat16),
            pltpu.VMEM((total, half), jnp.float32),
            pltpu.SemaphoreType.DMA((total // block,)),
            pltpu.SemaphoreType.DMA,
        ],
        compiler_params=pltpu.CompilerParams(vmem_limit_bytes=24 * MIB),
        name="pool",
    )(train_windows, test_windows, weight, gain, cls_t, train_labels, test_labels)


def sign_kernel(seed_ref, sign_ref, turned):
    proj_index = lax.axis_index("proj")
    parts, rows, part_width = sign_ref.shape
    count = parts * part_width
    chunks = rows // 128
    per_chunk = 128 // NCLS
    turned[:, pl.ds(0, chunks)] = seed_ref[...].T
    columns = (
        lax.broadcasted_iota(jnp.int32, (per_chunk, count), 1) + proj_index * count
    ) * MIX_COLUMN
    for k in range(NCLS):
        seeds = turned[pl.ds(k, per_chunk, stride=NCLS), :]
        for h in range(chunks):
            mixed = (seeds[:, h : h + 1] ^ columns) * MIX_FIRST
            mixed = (mixed ^ (mixed >> 13)) * MIX_LAST
            signs = jnp.where(mixed < 0, -1.0, 1.0).astype(jnp.bfloat16)
            at = (k * chunks + h) * per_chunk
            for n in range(parts):
                sign_ref[n, pl.ds(at, per_chunk), :] = signs[:, n * part_width : (n + 1) * part_width]


def sign_block(seeds, count):
    rows = seeds.shape[0]
    parts = count // 256
    return pl.pallas_call(
        sign_kernel,
        out_shape=jax.ShapeDtypeStruct((parts, rows, 256), jnp.bfloat16),
        in_specs=[VMEM],
        out_specs=VMEM,
        scratch_shapes=[pltpu.VMEM((128, 128), jnp.int32)],
        compiler_params=pltpu.CompilerParams(vmem_limit_bytes=16 * MIB),
        cost_estimate=pl.CostEstimate(flops=8 * rows * count, bytes_accessed=2 * rows * count, transcendentals=0),
        name="signs",
    )(seeds.reshape(rows // 128, 128))


def score_kernel(train_blocks, test_blocks, train_count, test_count, *refs):
    packets = refs[: 2 * (train_blocks + test_blocks)]
    own_signs, other_signs, precond_ref, keep_ref, send_ref, grad, row_weight, total = refs[
        2 * (train_blocks + test_blocks) :
    ]
    step = pl.program_id(0)
    proj_index = lax.axis_index("proj")
    half = packets[0].shape[1]
    part_width = own_signs.shape[2]
    train_rows = train_blocks * train_count
    half_rows = NCLS * half

    @pl.when(step == 0)
    def _():
        total[...] = jnp.zeros_like(total)
        for i in range(train_blocks + test_blocks):
            mine, theirs = packets[2 * i], packets[2 * i + 1]
            if i < train_blocks:
                count = train_count
                at = _source(lax.axis_index("train"), i, train_blocks) * count
            else:
                count = test_count
                at = train_rows + _source(
                    lax.axis_index("test"), i - train_blocks, test_blocks
                ) * count
            at = pl.multiple_of(at, count)
            logits = mine[pl.ds(count, NCLS), pl.ds(0, 128)] + theirs[pl.ds(count, NCLS), pl.ds(0, 128)]
            label = mine[pl.ds(count, NCLS), pl.ds(128, 128)]
            chance = 1.0 / (1.0 + jnp.exp(-logits))
            classes = lax.broadcasted_iota(jnp.int32, (NCLS, 128), 0).astype(jnp.float32)
            target = jnp.where(label == classes, 1.0, 0.0)
            retain = 1.0 - jnp.sum(chance * target, axis=0, keepdims=True)
            stacked = jnp.concatenate(
                [chance - target, jnp.broadcast_to(retain, (NCLS, 128))], axis=0
            )
            turned = stacked.T[:count]
            if i < train_blocks:
                row_weight[pl.ds(at, count), :] = jnp.broadcast_to(turned[:, NCLS : NCLS + 1], (count, 128))
            for side, packet in enumerate((mine, theirs)):
                value = packet[pl.ds(0, count), :]
                for k in range(NCLS):
                    grad[pl.ds(at, count), pl.ds(side * half_rows + k * half, half)] = (
                        value * turned[:, k : k + 1]
                    ).astype(jnp.bfloat16)

    projected = jnp.dot(
        grad[:, pl.ds(0, half_rows)], own_signs[0], preferred_element_type=jnp.float32
    ) + jnp.dot(
        grad[:, pl.ds(half_rows, half_rows)], other_signs[0], preferred_element_type=jnp.float32
    )
    weight = row_weight[...]
    train_feat = (
        projected[:train_rows] * jnp.concatenate([weight] * (part_width // 128), axis=1)
    ).astype(jnp.bfloat16)
    test_feat = (projected[train_rows:] * precond_ref[...]).astype(jnp.bfloat16)
    total[...] += lax.dot_general(
        test_feat,
        train_feat,
        (((1,), (1,)), ((), ())),
        preferred_element_type=jnp.float32,
    )

    @pl.when(step == pl.num_programs(0) - 1)
    def _():
        out_width = keep_ref.shape[1]
        keep_ref[...] = total[:, pl.ds(pl.multiple_of(proj_index * out_width, 128), out_width)]
        send_ref[...] = total[:, pl.ds(pl.multiple_of((1 - proj_index) * out_width, 128), out_width)]


def _source(index, shift, count):
    if count & (count - 1) == 0:
        return index ^ shift
    return lax.rem(index + count - shift, count)


def _pairs(shift, count):
    if count & (count - 1) == 0:
        return [(i, i ^ shift) for i in range(count)]
    return [(i, (i + shift) % count) for i in range(count)]


def partial_scores(packets, own_signs, other_signs, precond, train_blocks, test_blocks, train_count, test_count):
    parts, rows, part_width = own_signs.shape
    total_rows = train_blocks * train_count + test_blocks * test_count
    out_rows = test_blocks * test_count
    out_cols = train_blocks * train_count
    sign_spec = pl.BlockSpec((1, rows, part_width), lambda n: (n, 0, 0))
    packet_specs = [pl.BlockSpec(v.shape, lambda n: (0, 0)) for v in packets]
    out_spec = pl.BlockSpec((out_rows, out_cols // 2), lambda n: (0, 0))
    return pl.pallas_call(
        functools.partial(score_kernel, train_blocks, test_blocks, train_count, test_count),
        grid=(parts,),
        out_shape=(jax.ShapeDtypeStruct((out_rows, out_cols // 2), jnp.float32),) * 2,
        in_specs=packet_specs
        + [
            sign_spec,
            sign_spec,
            pl.BlockSpec(
                (1, part_width), lambda n: (0, lax.axis_index("proj") * parts + n)
            ),
        ],
        out_specs=(out_spec, out_spec),
        scratch_shapes=[
            pltpu.VMEM((total_rows, 2 * rows), jnp.bfloat16),
            pltpu.VMEM((out_cols, 128), jnp.float32),
            pltpu.VMEM((out_rows, out_cols), jnp.float32),
        ],
        compiler_params=pltpu.CompilerParams(vmem_limit_bytes=40 * MIB),
        name="partial_scores",
    )(*packets, own_signs, other_signs, precond)


def shards(
    train_windows,
    test_windows,
    train_labels,
    test_labels,
    dilated_weight,
    branch_gain,
    cls_weight,
    sign_seeds,
    precond,
):
    train_count = train_windows.shape[0]
    test_count = test_windows.shape[0]
    train_blocks = lax.axis_size("train")
    test_blocks = lax.axis_size("test")
    count = K // lax.axis_size("proj")
    swap = [(0, 1), (1, 0)]
    other_seeds = lax.ppermute(sign_seeds, "proj", swap)
    train_packet, test_packet = pool(
        train_windows,
        test_windows,
        dilated_weight,
        branch_gain.reshape(1, -1),
        cls_weight.T,
        train_labels.reshape(1, -1),
        test_labels.reshape(1, -1),
    )
    mine = [train_packet]
    for shift in range(1, train_blocks):
        mine.append(lax.ppermute(train_packet, "train", _pairs(shift, train_blocks)))
    mine.append(test_packet)
    for shift in range(1, test_blocks):
        mine.append(lax.ppermute(test_packet, "test", _pairs(shift, test_blocks)))
    own_signs = sign_block(sign_seeds, count)
    other_signs = sign_block(other_seeds, count)
    packets = []
    for value in mine:
        packets += [value, lax.ppermute(value, "proj", swap)]
    keep, send = partial_scores(
        packets,
        own_signs,
        other_signs,
        precond.reshape(1, -1),
        train_blocks,
        test_blocks,
        train_count,
        test_count,
    )
    received = lax.ppermute(send, "proj", swap)
    return (keep + received) * (1.0 / (K * math.sqrt(C)))


def solution(mesh):
    return jax.shard_map(
        shards,
        mesh=mesh,
        in_specs=(
            P(("grp", "test", "train"), None, None),
            P(("grp", "train", "test"), None, None),
            P(("grp", "test", "train")),
            P(("grp", "train", "test")),
            P(None, None, "proj"),
            P("proj"),
            P("proj", None),
            P("proj"),
            P(),
        ),
        out_specs=P(("grp", "train"), ("test", "proj")),
        check_vma=False,
    )
```

```python
import functools
import math

import jax
import jax.numpy as jnp
from jax import lax
from jax.experimental import pallas as pl
from jax.experimental.pallas import tpu as pltpu
from jax.sharding import PartitionSpec as P

C = 512
NCLS = 8
K = 2048
DILATION_STEP = 4
MIX_COLUMN = 668265261
MIX_FIRST = 625341585
MIX_LAST = (1274126177 << 15) & 0xFFFFFFFF
MIX_LAST = MIX_LAST - (1 << 32) if MIX_LAST >= 1 << 31 else MIX_LAST
MIB = 2**20

VMEM = pl.BlockSpec(memory_space=pltpu.VMEM)
HBM = pl.BlockSpec(memory_space=pltpu.HBM)


def pool_kernel(
    block,
    train_hbm,
    test_hbm,
    weight_hbm,
    gain_ref,
    cls_ref,
    train_label_ref,
    test_label_ref,
    seed_ref,
    train_packet,
    test_packet,
    own_packet,
    rows,
    weight,
    pooled,
    gain_row,
    cls_rows,
    train_label,
    test_label,
    seeds,
    row_sem,
    weight_sem,
    small_sem,
):
    proj_index = lax.axis_index("proj")
    train_count, length, width = train_hbm.shape
    test_count = test_hbm.shape[0]
    half = weight.shape[2]
    blocks = (train_count + test_count) // block
    weight_copy = pltpu.make_async_copy(weight_hbm, weight, weight_sem)
    weight_copy.start()
    for b in range(blocks):
        source = train_hbm if b < train_count // block else test_hbm
        offset = b * block if b < train_count // block else b * block - train_count
        pltpu.make_async_copy(
            source.at[pl.ds(offset, block)], rows.at[pl.ds(b * block, block)], row_sem.at[b]
        ).start()
    small = [
        pltpu.make_async_copy(source, target, small_sem.at[i])
        for i, (source, target) in enumerate(
            (
                (gain_ref, gain_row),
                (cls_ref, cls_rows),
                (train_label_ref, train_label),
                (test_label_ref, test_label),
                (seed_ref, seeds),
            )
        )
    ]
    for copy in small:
        copy.start()
    weight_copy.wait()
    for copy in small:
        copy.wait()
    gain = gain_row[...]
    own_start = pl.multiple_of(proj_index * half, half)

    def one_block(b, carry):
        start = b * block
        pltpu.make_async_copy(
            test_hbm.at[pl.ds(0, block)], rows.at[pl.ds(start, block)], row_sem.at[b]
        ).wait()
        x = rows[pl.ds(start, block)]
        zeros = jnp.zeros((block, DILATION_STEP, width), x.dtype)
        before = jnp.concatenate([zeros, x[:, : length - DILATION_STEP]], axis=1)
        after = jnp.concatenate([x[:, DILATION_STEP:], zeros], axis=1)
        taps = jnp.concatenate([before, x, after], axis=2).reshape(block * length, 3 * width)
        conv = jnp.dot(
            taps, weight[...].reshape(3 * width, half), preferred_element_type=jnp.float32
        ).reshape(block, length, half)
        own = rows[pl.ds(start, block), :, pl.ds(own_start, half)].astype(jnp.float32)
        total = jnp.sum(own, axis=1) + gain * jnp.sum(jnp.maximum(conv, 0.0), axis=1)
        pooled[pl.ds(pl.multiple_of(start, block), block), :] = total * (1.0 / length)
        return carry

    lax.fori_loop(0, blocks, one_block, 0)
    at = 0
    for packet, label_ref, start, count in (
        (train_packet, train_label, 0, train_count),
        (test_packet, test_label, train_count, test_count),
    ):
        own = pooled[pl.ds(start, count), :]
        logits = lax.dot_general(
            cls_rows[...],
            own,
            (((1,), (1,)), ((), ())),
            precision=lax.Precision.HIGHEST,
            preferred_element_type=jnp.float32,
        )
        labels = jnp.broadcast_to(label_ref[...].astype(jnp.float32), (NCLS, count))
        for target, first in ((packet, 0), (own_packet, at)):
            target[pl.ds(first, count), :] = own
            target[pl.ds(first + count, NCLS), pl.ds(0, count)] = logits
            target[pl.ds(first + count, NCLS), pl.ds(128, count)] = labels
        at += count + NCLS
    own_packet[pl.ds(at, seeds.shape[0]), pl.ds(0, 128)] = (seeds[...] >> 15).astype(jnp.float32)
    own_packet[pl.ds(at, seeds.shape[0]), pl.ds(128, 128)] = (seeds[...] & 32767).astype(jnp.float32)


def pool(train_windows, test_windows, weight, gain, cls_t, train_labels, test_labels, seeds):
    block = 8
    train_count, length, width = train_windows.shape
    test_count = test_windows.shape[0]
    half = weight.shape[2]
    total = train_count + test_count
    return pl.pallas_call(
        functools.partial(pool_kernel, block),
        out_shape=(
            jax.ShapeDtypeStruct((train_count + NCLS, half), jnp.float32),
            jax.ShapeDtypeStruct((test_count + NCLS, half), jnp.float32),
            jax.ShapeDtypeStruct((total + 2 * NCLS + seeds.shape[0], half), jnp.float32),
        ),
        in_specs=[HBM] * 8,
        out_specs=(VMEM, VMEM, VMEM),
        scratch_shapes=[
            pltpu.VMEM((total, length, width), jnp.bfloat16),
            pltpu.VMEM(weight.shape, jnp.bfloat16),
            pltpu.VMEM((total, half), jnp.float32),
            pltpu.VMEM(gain.shape, jnp.float32),
            pltpu.VMEM(cls_t.shape, jnp.float32),
            pltpu.VMEM(train_labels.shape, jnp.int32),
            pltpu.VMEM(test_labels.shape, jnp.int32),
            pltpu.VMEM(seeds.shape, jnp.int32),
            pltpu.SemaphoreType.DMA((total // block,)),
            pltpu.SemaphoreType.DMA,
            pltpu.SemaphoreType.DMA((5,)),
        ],
        compiler_params=pltpu.CompilerParams(vmem_limit_bytes=24 * MIB),
        name="pool",
    )(
        *(
            pltpu.with_memory_space_constraint(value, pltpu.HBM)
            for value in (train_windows, test_windows, weight, gain, cls_t, train_labels, test_labels, seeds)
        )
    )


def sign_kernel(packed, seed_ref, sign_ref, turned):
    proj_index = lax.axis_index("proj")
    parts, rows, part_width = sign_ref.shape
    count = parts * part_width
    chunks = rows // 128
    per_chunk = 128 // NCLS
    if packed:
        first = seed_ref.shape[0] - chunks
        high = seed_ref[pl.ds(first, chunks), pl.ds(0, 128)].astype(jnp.int32)
        seeds = high * 32768 + seed_ref[pl.ds(first, chunks), pl.ds(128, 128)].astype(jnp.int32)
    else:
        seeds = seed_ref[...]
    turned[:, pl.ds(0, chunks)] = seeds.T
    columns = (
        lax.broadcasted_iota(jnp.int32, (per_chunk, count), 1) + proj_index * count
    ) * MIX_COLUMN
    for k in range(NCLS):
        seeds = turned[pl.ds(k, per_chunk, stride=NCLS), :]
        for h in range(chunks):
            mixed = (seeds[:, h : h + 1] ^ columns) * MIX_FIRST
            mixed = (mixed ^ (mixed >> 13)) * MIX_LAST
            signs = jnp.where(mixed < 0, -1.0, 1.0).astype(jnp.bfloat16)
            at = (k * chunks + h) * per_chunk
            for n in range(parts):
                sign_ref[n, pl.ds(at, per_chunk), :] = signs[:, n * part_width : (n + 1) * part_width]


def sign_block(seeds, rows, count):
    parts = count // 256
    return pl.pallas_call(
        functools.partial(sign_kernel, seeds.dtype == jnp.float32),
        out_shape=jax.ShapeDtypeStruct((parts, rows, 256), jnp.bfloat16),
        in_specs=[VMEM],
        out_specs=VMEM,
        scratch_shapes=[pltpu.VMEM((128, 128), jnp.int32)],
        compiler_params=pltpu.CompilerParams(vmem_limit_bytes=16 * MIB),
        cost_estimate=pl.CostEstimate(
            flops=8 * rows * count, bytes_accessed=2 * rows * count, transcendentals=0
        ),
        name="signs",
    )(seeds)


def score_kernel(train_blocks, test_blocks, train_count, test_count, *refs):
    far = train_blocks + test_blocks - 2
    packets = refs[: 2 * far + 2]
    own_signs, other_signs, precond_ref, keep_ref, send_ref, grad, row_weight, total = refs[2 * far + 2 :]
    step = pl.program_id(0)
    proj_index = lax.axis_index("proj")
    half = packets[0].shape[1]
    part_width = own_signs.shape[2]
    train_rows = train_blocks * train_count
    half_rows = NCLS * half

    @pl.when(step == 0)
    def _():
        total[...] = jnp.zeros_like(total)
        for i in range(train_blocks + test_blocks):
            first = 0
            if i == 0:
                mine, theirs = packets[0], packets[1]
            elif i < train_blocks:
                mine, theirs = packets[2 * i], packets[2 * i + 1]
            elif i == train_blocks:
                mine, theirs = packets[0], packets[1]
                first = train_count + NCLS
            else:
                mine, theirs = packets[2 * (i - 1)], packets[2 * (i - 1) + 1]
            if i < train_blocks:
                count = train_count
                at = _source(lax.axis_index("train"), i, train_blocks) * count
            else:
                count = test_count
                at = train_rows + _source(
                    lax.axis_index("test"), i - train_blocks, test_blocks
                ) * count
            at = pl.multiple_of(at, count)
            class_rows = pl.ds(first + count, NCLS)
            logits = mine[class_rows, pl.ds(0, 128)] + theirs[class_rows, pl.ds(0, 128)]
            label = mine[class_rows, pl.ds(128, 128)]
            chance = 1.0 / (1.0 + jnp.exp(-logits))
            classes = lax.broadcasted_iota(jnp.int32, (NCLS, 128), 0).astype(jnp.float32)
            target = jnp.where(label == classes, 1.0, 0.0)
            retain = 1.0 - jnp.sum(chance * target, axis=0, keepdims=True)
            stacked = jnp.concatenate(
                [chance - target, jnp.broadcast_to(retain, (NCLS, 128))], axis=0
            )
            turned = stacked.T[:count]
            if i < train_blocks:
                row_weight[pl.ds(at, count), :] = jnp.broadcast_to(turned[:, NCLS : NCLS + 1], (count, 128))
            for side, packet in enumerate((mine, theirs)):
                value = packet[pl.ds(first, count), :]
                for k in range(NCLS):
                    grad[pl.ds(at, count), pl.ds(side * half_rows + k * half, half)] = (
                        value * turned[:, k : k + 1]
                    ).astype(jnp.bfloat16)

    projected = jnp.dot(
        grad[:, pl.ds(0, half_rows)], own_signs[0], preferred_element_type=jnp.float32
    ) + jnp.dot(
        grad[:, pl.ds(half_rows, half_rows)], other_signs[0], preferred_element_type=jnp.float32
    )
    weight = row_weight[...]
    train_feat = (
        projected[:train_rows] * jnp.concatenate([weight] * (part_width // 128), axis=1)
    ).astype(jnp.bfloat16)
    test_feat = (projected[train_rows:] * precond_ref[...]).astype(jnp.bfloat16)
    total[...] += lax.dot_general(
        test_feat,
        train_feat,
        (((1,), (1,)), ((), ())),
        preferred_element_type=jnp.float32,
    )

    @pl.when(step == pl.num_programs(0) - 1)
    def _():
        out_width = keep_ref.shape[1]
        keep_ref[...] = total[:, pl.ds(pl.multiple_of(proj_index * out_width, 128), out_width)]
        send_ref[...] = total[:, pl.ds(pl.multiple_of((1 - proj_index) * out_width, 128), out_width)]


def _source(index, shift, count):
    if count & (count - 1) == 0:
        return index ^ shift
    return lax.rem(index + count - shift, count)


def _pairs(shift, count):
    if count & (count - 1) == 0:
        return [(i, i ^ shift) for i in range(count)]
    return [(i, (i + shift) % count) for i in range(count)]


def partial_scores(packets, own_signs, other_signs, precond, train_blocks, test_blocks, train_count, test_count):
    parts, rows, part_width = own_signs.shape
    total_rows = train_blocks * train_count + test_blocks * test_count
    out_rows = test_blocks * test_count
    out_cols = train_blocks * train_count
    sign_spec = pl.BlockSpec((1, rows, part_width), lambda n: (n, 0, 0))
    packet_specs = [pl.BlockSpec(v.shape, lambda n: (0, 0)) for v in packets]
    out_spec = pl.BlockSpec((out_rows, out_cols // 2), lambda n: (0, 0))
    return pl.pallas_call(
        functools.partial(score_kernel, train_blocks, test_blocks, train_count, test_count),
        grid=(parts,),
        out_shape=(jax.ShapeDtypeStruct((out_rows, out_cols // 2), jnp.float32),) * 2,
        in_specs=packet_specs
        + [
            sign_spec,
            sign_spec,
            pl.BlockSpec(
                (1, part_width), lambda n: (0, lax.axis_index("proj") * parts + n)
            ),
        ],
        out_specs=(out_spec, out_spec),
        scratch_shapes=[
            pltpu.VMEM((total_rows, 2 * rows), jnp.bfloat16),
            pltpu.VMEM((out_cols, 128), jnp.float32),
            pltpu.VMEM((out_rows, out_cols), jnp.float32),
        ],
        compiler_params=pltpu.CompilerParams(vmem_limit_bytes=40 * MIB),
        name="partial_scores",
    )(*packets, own_signs, other_signs, precond)


def shards(
    train_windows,
    test_windows,
    train_labels,
    test_labels,
    dilated_weight,
    branch_gain,
    cls_weight,
    sign_seeds,
    precond,
):
    train_count = train_windows.shape[0]
    test_count = test_windows.shape[0]
    train_blocks = lax.axis_size("train")
    test_blocks = lax.axis_size("test")
    count = K // lax.axis_size("proj")
    swap = [(0, 1), (1, 0)]
    seeds = sign_seeds.reshape(-1, 128)
    train_packet, test_packet, own_packet = pool(
        train_windows,
        test_windows,
        dilated_weight,
        branch_gain.reshape(1, -1),
        cls_weight.T,
        train_labels.reshape(1, -1),
        test_labels.reshape(1, -1),
        seeds,
    )
    far = [lax.ppermute(train_packet, "train", _pairs(shift, train_blocks)) for shift in range(1, train_blocks)]
    far += [lax.ppermute(test_packet, "test", _pairs(shift, test_blocks)) for shift in range(1, test_blocks)]
    other_packet = lax.ppermute(own_packet, "proj", swap)
    own_signs = sign_block(seeds, sign_seeds.shape[0], count)
    *far, own_signs, other_packet = lax.optimization_barrier((*far, own_signs, other_packet))
    other_signs = sign_block(other_packet, sign_seeds.shape[0], count)
    packets = [own_packet, other_packet]
    for value in far:
        packets += [value, lax.ppermute(value, "proj", swap)]
    keep, send = partial_scores(
        packets,
        own_signs,
        other_signs,
        precond.reshape(1, -1),
        train_blocks,
        test_blocks,
        train_count,
        test_count,
    )
    received = lax.ppermute(send, "proj", swap)
    return (keep + received) * (1.0 / (K * math.sqrt(C)))


def solution(mesh):
    return jax.shard_map(
        shards,
        mesh=mesh,
        in_specs=(
            P(("grp", "test", "train"), None, None),
            P(("grp", "train", "test"), None, None),
            P(("grp", "test", "train")),
            P(("grp", "train", "test")),
            P(None, None, "proj"),
            P("proj"),
            P("proj", None),
            P("proj"),
            P(),
        ),
        out_specs=P(("grp", "train"), ("test", "proj")),
        check_vma=False,
    )
```

```python
import functools
import math

import jax
import jax.numpy as jnp
from jax import lax
from jax.experimental import pallas as pl
from jax.experimental.pallas import tpu as pltpu
from jax.sharding import PartitionSpec as P

C = 512
NCLS = 8
K = 2048
DILATION_STEP = 4
MIX_COLUMN = 668265261
MIX_FIRST = 625341585
MIX_LAST = (1274126177 << 15) & 0xFFFFFFFF
MIX_LAST = MIX_LAST - (1 << 32) if MIX_LAST >= 1 << 31 else MIX_LAST
MIB = 2**20
AHEAD = 3

VMEM = pl.BlockSpec(memory_space=pltpu.VMEM)
HBM = pl.BlockSpec(memory_space=pltpu.HBM)


def pool_kernel(
    block,
    train_hbm,
    test_hbm,
    weight_hbm,
    gain_ref,
    cls_ref,
    train_label_ref,
    test_label_ref,
    seed_ref,
    train_packet,
    test_packet,
    own_packet,
    rows,
    weight,
    pooled,
    gain_row,
    cls_rows,
    train_label,
    test_label,
    seeds,
    row_sem,
    weight_sem,
    small_sem,
):
    proj_index = lax.axis_index("proj")
    train_count, length, width = train_hbm.shape
    test_count = test_hbm.shape[0]
    half = weight.shape[2]
    blocks = (train_count + test_count) // block
    weight_copy = pltpu.make_async_copy(weight_hbm, weight, weight_sem)
    weight_copy.start()

    def fetch(b):
        source = train_hbm if b < train_count // block else test_hbm
        offset = b * block if b < train_count // block else b * block - train_count
        return pltpu.make_async_copy(
            source.at[pl.ds(offset, block)], rows.at[pl.ds(b * block, block)], row_sem.at[b]
        )

    for b in range(min(AHEAD, blocks)):
        fetch(b).start()
    small = [
        pltpu.make_async_copy(source, target, small_sem.at[i])
        for i, (source, target) in enumerate(
            (
                (gain_ref, gain_row),
                (cls_ref, cls_rows),
                (train_label_ref, train_label),
                (test_label_ref, test_label),
                (seed_ref, seeds),
            )
        )
    ]
    for copy in small:
        copy.start()
    weight_copy.wait()
    for copy in small:
        copy.wait()
    gain = gain_row[...]
    own_start = pl.multiple_of(proj_index * half, half)

    def one_block(b, carry):
        start = b * block
        for late in range(AHEAD, blocks):

            @pl.when(b == late - AHEAD)
            def _():
                fetch(late).start()

        pltpu.make_async_copy(
            test_hbm.at[pl.ds(0, block)], rows.at[pl.ds(start, block)], row_sem.at[b]
        ).wait()
        x = rows[pl.ds(start, block)]
        zeros = jnp.zeros((block, DILATION_STEP, width), x.dtype)
        before = jnp.concatenate([zeros, x[:, : length - DILATION_STEP]], axis=1)
        after = jnp.concatenate([x[:, DILATION_STEP:], zeros], axis=1)
        taps = jnp.concatenate([before, x, after], axis=2).reshape(block * length, 3 * width)
        conv = jnp.dot(
            taps, weight[...].reshape(3 * width, half), preferred_element_type=jnp.float32
        ).reshape(block, length, half)
        own = rows[pl.ds(start, block), :, pl.ds(own_start, half)].astype(jnp.float32)
        total = jnp.sum(own, axis=1) + gain * jnp.sum(jnp.maximum(conv, 0.0), axis=1)
        pooled[pl.ds(pl.multiple_of(start, block), block), :] = total * (1.0 / length)
        return carry

    lax.fori_loop(0, blocks, one_block, 0)
    at = 0
    for packet, label_ref, start, count in (
        (train_packet, train_label, 0, train_count),
        (test_packet, test_label, train_count, test_count),
    ):
        own = pooled[pl.ds(start, count), :]
        logits = lax.dot_general(
            cls_rows[...],
            own,
            (((1,), (1,)), ((), ())),
            precision=lax.Precision.HIGHEST,
            preferred_element_type=jnp.float32,
        )
        labels = jnp.broadcast_to(label_ref[...].astype(jnp.float32), (NCLS, count))
        for target, first in ((packet, 0), (own_packet, at)):
            target[pl.ds(first, count), :] = own
            target[pl.ds(first + count, NCLS), pl.ds(0, count)] = logits
            target[pl.ds(first + count, NCLS), pl.ds(128, count)] = labels
        at += count + NCLS
    own_packet[pl.ds(at, seeds.shape[0]), pl.ds(0, 128)] = (seeds[...] >> 15).astype(jnp.float32)
    own_packet[pl.ds(at, seeds.shape[0]), pl.ds(128, 128)] = (seeds[...] & 32767).astype(jnp.float32)


def pool(train_windows, test_windows, weight, gain, cls_t, train_labels, test_labels, seeds):
    block = 16
    train_count, length, width = train_windows.shape
    test_count = test_windows.shape[0]
    half = weight.shape[2]
    total = train_count + test_count
    return pl.pallas_call(
        functools.partial(pool_kernel, block),
        out_shape=(
            jax.ShapeDtypeStruct((train_count + NCLS, half), jnp.float32),
            jax.ShapeDtypeStruct((test_count + NCLS, half), jnp.float32),
            jax.ShapeDtypeStruct((total + 2 * NCLS + seeds.shape[0], half), jnp.float32),
        ),
        in_specs=[HBM] * 8,
        out_specs=(VMEM, VMEM, VMEM),
        scratch_shapes=[
            pltpu.VMEM((total, length, width), jnp.bfloat16),
            pltpu.VMEM(weight.shape, jnp.bfloat16),
            pltpu.VMEM((total, half), jnp.float32),
            pltpu.VMEM(gain.shape, jnp.float32),
            pltpu.VMEM(cls_t.shape, jnp.float32),
            pltpu.VMEM(train_labels.shape, jnp.int32),
            pltpu.VMEM(test_labels.shape, jnp.int32),
            pltpu.VMEM(seeds.shape, jnp.int32),
            pltpu.SemaphoreType.DMA((total // block,)),
            pltpu.SemaphoreType.DMA,
            pltpu.SemaphoreType.DMA((5,)),
        ],
        compiler_params=pltpu.CompilerParams(vmem_limit_bytes=24 * MIB),
        name="pool",
    )(
        *(
            pltpu.with_memory_space_constraint(value, pltpu.HBM)
            for value in (train_windows, test_windows, weight, gain, cls_t, train_labels, test_labels, seeds)
        )
    )


def sign_kernel(packed, seed_ref, sign_ref, turned, column_ref):
    proj_index = lax.axis_index("proj")
    parts, rows, part_width = sign_ref.shape
    count = parts * part_width
    chunks = rows // 128
    per_chunk = 128 // NCLS
    if packed:
        first = seed_ref.shape[0] - chunks
        high = seed_ref[pl.ds(first, chunks), pl.ds(0, 128)].astype(jnp.int32)
        seeds = high * 32768 + seed_ref[pl.ds(first, chunks), pl.ds(128, 128)].astype(jnp.int32)
    else:
        seeds = seed_ref[...]
    turned[:, pl.ds(0, chunks)] = seeds.T

    @pl.when(proj_index >= 0)
    def _():
        column_ref[...] = (
            lax.broadcasted_iota(jnp.int32, column_ref.shape, 1) + proj_index * count
        ) * MIX_COLUMN

    for k in range(NCLS):
        seeds = turned[pl.ds(k, per_chunk, stride=NCLS), :]
        for h in range(chunks):
            mixed = (seeds[:, h : h + 1] ^ column_ref[...]) * MIX_FIRST
            mixed = (mixed ^ (mixed >> 13)) * MIX_LAST
            signs = jnp.where(mixed < 0, -1.0, 1.0).astype(jnp.bfloat16)
            at = (k * chunks + h) * per_chunk
            for n in range(parts):
                sign_ref[n, pl.ds(at, per_chunk), :] = signs[:, n * part_width : (n + 1) * part_width]


def sign_block(seeds, rows, count):
    parts = count // 256
    return pl.pallas_call(
        functools.partial(sign_kernel, seeds.dtype == jnp.float32),
        out_shape=jax.ShapeDtypeStruct((parts, rows, 256), jnp.bfloat16),
        in_specs=[VMEM],
        out_specs=VMEM,
        scratch_shapes=[pltpu.VMEM((128, 128), jnp.int32), pltpu.VMEM((128 // NCLS, count), jnp.int32)],
        compiler_params=pltpu.CompilerParams(vmem_limit_bytes=16 * MIB),
        cost_estimate=pl.CostEstimate(
            flops=8 * rows * count, bytes_accessed=2 * rows * count, transcendentals=0
        ),
        name="signs",
    )(seeds)


def score_kernel(train_blocks, test_blocks, train_count, test_count, *refs):
    far = train_blocks + test_blocks - 2
    packets = refs[: 2 * far + 2]
    own_signs, other_signs, precond_ref, keep_ref, send_ref, train_feat, test_feat = refs[2 * far + 2 :]
    proj_index = lax.axis_index("proj")
    parts, half_rows, part_width = own_signs.shape
    train_rows = train_blocks * train_count
    gradients = []
    row_weights = []
    for i in range(train_blocks + test_blocks):
        first = 0
        if i == 0:
            mine, theirs = packets[0], packets[1]
        elif i < train_blocks:
            mine, theirs = packets[2 * i], packets[2 * i + 1]
        elif i == train_blocks:
            mine, theirs = packets[0], packets[1]
            first = train_count + NCLS
        else:
            mine, theirs = packets[2 * (i - 1)], packets[2 * (i - 1) + 1]
        count = train_count if i < train_blocks else test_count
        class_rows = pl.ds(first + count, NCLS)
        logits = mine[class_rows, pl.ds(0, 128)] + theirs[class_rows, pl.ds(0, 128)]
        label = mine[class_rows, pl.ds(128, 128)]
        chance = 1.0 / (1.0 + jnp.exp(-logits))
        classes = lax.broadcasted_iota(jnp.int32, (NCLS, 128), 0).astype(jnp.float32)
        target = jnp.where(label == classes, 1.0, 0.0)
        retain = 1.0 - jnp.sum(chance * target, axis=0, keepdims=True)
        stacked = jnp.concatenate([chance - target, jnp.broadcast_to(retain, (NCLS, 128))], axis=0)
        turned = stacked.T[:count]
        if i < train_blocks:
            row_weights.append(turned[:, NCLS : NCLS + 1])
        pieces = []
        for packet in (mine, theirs):
            value = packet[pl.ds(first, count), :]
            for k in range(NCLS):
                pieces.append((value * turned[:, k : k + 1]).astype(jnp.bfloat16))
        gradients.append(jnp.concatenate(pieces, axis=1))
    gradient = jnp.concatenate(gradients, axis=0)
    train_index, test_index = lax.axis_index("train"), lax.axis_index("test")
    for n in range(parts):
        projected = jnp.dot(
            gradient,
            jnp.concatenate([own_signs[n], other_signs[n]], axis=0),
            preferred_element_type=jnp.float32,
        )
        columns = pl.ds(n * part_width, part_width)
        for i in range(train_blocks):
            part = projected[i * train_count : (i + 1) * train_count]
            train_feat[_source(train_index, i, train_blocks), :, columns] = (
                part * row_weights[i]
            ).astype(jnp.bfloat16)
        precond = precond_ref[
            :, pl.ds(pl.multiple_of(proj_index * (parts * part_width) + n * part_width, 128), part_width)
        ]
        for i in range(test_blocks):
            start = train_rows + i * test_count
            test_feat[_source(test_index, i, test_blocks), :, columns] = (
                projected[start : start + test_count] * precond
            ).astype(jnp.bfloat16)
    half_blocks = train_blocks // 2
    test = test_feat[...].reshape(test_blocks * test_count, parts * part_width)
    for target, side in ((send_ref, 1 - proj_index), (keep_ref, proj_index)):
        train = train_feat[pl.ds(side * half_blocks, half_blocks)].reshape(
            half_blocks * train_count, parts * part_width
        )
        target[...] = lax.dot_general(
            test, train, (((1,), (1,)), ((), ())), preferred_element_type=jnp.float32
        )


def _source(index, shift, count):
    if count & (count - 1) == 0:
        return index ^ shift
    return lax.rem(index + count - shift, count)


def _pairs(shift, count):
    if count & (count - 1) == 0:
        return [(i, i ^ shift) for i in range(count)]
    return [(i, (i + shift) % count) for i in range(count)]


def partial_scores(packets, own_signs, other_signs, precond, train_blocks, test_blocks, train_count, test_count):
    parts, rows, part_width = own_signs.shape
    out_rows = test_blocks * test_count
    out_cols = train_blocks * train_count
    total_rows = out_rows + out_cols
    return pl.pallas_call(
        functools.partial(score_kernel, train_blocks, test_blocks, train_count, test_count),
        out_shape=(jax.ShapeDtypeStruct((out_rows, out_cols // 2), jnp.float32),) * 2,
        in_specs=[VMEM] * (len(packets) + 3),
        out_specs=(VMEM, VMEM),
        scratch_shapes=[
            pltpu.VMEM((train_blocks, train_count, parts * part_width), jnp.bfloat16),
            pltpu.VMEM((test_blocks, test_count, parts * part_width), jnp.bfloat16),
        ],
        compiler_params=pltpu.CompilerParams(vmem_limit_bytes=40 * MIB),
        cost_estimate=pl.CostEstimate(
            flops=4 * total_rows * rows * parts * part_width,
            bytes_accessed=4 * rows * parts * part_width,
            transcendentals=0,
        ),
        name="partial_scores",
    )(*packets, own_signs, other_signs, precond)


def shards(
    train_windows,
    test_windows,
    train_labels,
    test_labels,
    dilated_weight,
    branch_gain,
    cls_weight,
    sign_seeds,
    precond,
):
    train_count = train_windows.shape[0]
    test_count = test_windows.shape[0]
    train_blocks = lax.axis_size("train")
    test_blocks = lax.axis_size("test")
    count = K // lax.axis_size("proj")
    swap = [(0, 1), (1, 0)]
    seeds = sign_seeds.reshape(-1, 128)
    train_packet, test_packet, own_packet = pool(
        train_windows,
        test_windows,
        dilated_weight,
        branch_gain.reshape(1, -1),
        cls_weight.T,
        train_labels.reshape(1, -1),
        test_labels.reshape(1, -1),
        seeds,
    )
    far = [lax.ppermute(train_packet, "train", _pairs(shift, train_blocks)) for shift in range(1, train_blocks)]
    far += [lax.ppermute(test_packet, "test", _pairs(shift, test_blocks)) for shift in range(1, test_blocks)]
    other_packet = lax.ppermute(own_packet, "proj", swap)
    own_signs = sign_block(seeds, sign_seeds.shape[0], count)
    *far, own_signs, other_packet = lax.optimization_barrier((*far, own_signs, other_packet))
    other_signs = sign_block(other_packet, sign_seeds.shape[0], count)
    packets = [own_packet, other_packet]
    for value in far:
        packets += [value, lax.ppermute(value, "proj", swap)]
    keep, send = partial_scores(
        packets,
        own_signs,
        other_signs,
        precond.reshape(1, -1),
        train_blocks,
        test_blocks,
        train_count,
        test_count,
    )
    received = lax.ppermute(send, "proj", swap)
    return (keep + received) * (1.0 / (K * math.sqrt(C)))


def solution(mesh):
    return jax.shard_map(
        shards,
        mesh=mesh,
        in_specs=(
            P(("grp", "test", "train"), None, None),
            P(("grp", "train", "test"), None, None),
            P(("grp", "test", "train")),
            P(("grp", "train", "test")),
            P(None, None, "proj"),
            P("proj"),
            P("proj", None),
            P("proj"),
            P(),
        ),
        out_specs=P(("grp", "train"), ("test", "proj")),
        check_vma=False,
    )
```

```python
import functools
import math

import jax
import jax.numpy as jnp
from jax import lax
from jax.experimental import pallas as pl
from jax.experimental.pallas import tpu as pltpu
from jax.sharding import PartitionSpec as P

C = 512
NCLS = 8
K = 2048
DILATION_STEP = 4
MIX_COLUMN = 668265261
MIX_FIRST = 625341585
MIX_LAST = (1274126177 << 15) & 0xFFFFFFFF
MIX_LAST = MIX_LAST - (1 << 32) if MIX_LAST >= 1 << 31 else MIX_LAST
MIB = 2**20
AHEAD = 3

VMEM = pl.BlockSpec(memory_space=pltpu.VMEM)
HBM = pl.BlockSpec(memory_space=pltpu.HBM)


def pool_kernel(
    block,
    train_hbm,
    test_hbm,
    weight_hbm,
    gain_ref,
    cls_ref,
    train_label_ref,
    test_label_ref,
    seed_ref,
    train_packet,
    test_packet,
    own_packet,
    rows,
    weight,
    pooled,
    gain_row,
    cls_rows,
    train_label,
    test_label,
    seeds,
    row_sem,
    weight_sem,
    small_sem,
):
    proj_index = lax.axis_index("proj")
    train_count, length, width = train_hbm.shape
    test_count = test_hbm.shape[0]
    half = weight.shape[2]
    blocks = (train_count + test_count) // block
    small = [
        pltpu.make_async_copy(source, target, small_sem.at[i])
        for i, (source, target) in enumerate(
            (
                (gain_ref, gain_row),
                (cls_ref, cls_rows),
                (train_label_ref, train_label),
                (test_label_ref, test_label),
                (seed_ref, seeds),
            )
        )
    ]
    for copy in small:
        copy.start()
    weight_copy = pltpu.make_async_copy(weight_hbm, weight, weight_sem)
    weight_copy.start()

    def fetch(b):
        source = train_hbm if b < train_count // block else test_hbm
        offset = b * block if b < train_count // block else b * block - train_count
        return pltpu.make_async_copy(
            source.at[pl.ds(offset, block)], rows.at[pl.ds(b * block, block)], row_sem.at[b]
        )

    for b in range(min(AHEAD, blocks)):
        fetch(b).start()
    weight_copy.wait()
    for copy in small:
        copy.wait()
    gain = gain_row[...]
    own_start = pl.multiple_of(proj_index * half, half)

    def one_block(b, carry):
        start = b * block
        for late in range(AHEAD, blocks):

            @pl.when(b == late - AHEAD)
            def _():
                fetch(late).start()

        pltpu.make_async_copy(
            test_hbm.at[pl.ds(0, block)], rows.at[pl.ds(start, block)], row_sem.at[b]
        ).wait()
        x = rows[pl.ds(start, block)]
        zeros = jnp.zeros((block, DILATION_STEP, width), x.dtype)
        before = jnp.concatenate([zeros, x[:, : length - DILATION_STEP]], axis=1)
        after = jnp.concatenate([x[:, DILATION_STEP:], zeros], axis=1)
        taps = jnp.concatenate([before, x, after], axis=2).reshape(block * length, 3 * width)
        conv = jnp.dot(
            taps, weight[...].reshape(3 * width, half), preferred_element_type=jnp.float32
        ).reshape(block, length, half)
        own = rows[pl.ds(start, block), :, pl.ds(own_start, half)].astype(jnp.float32)
        total = jnp.sum(own, axis=1) + gain * jnp.sum(jnp.maximum(conv, 0.0), axis=1)
        pooled[pl.ds(pl.multiple_of(start, block), block), :] = total * (1.0 / length)
        return carry

    lax.fori_loop(0, blocks, one_block, 0)
    at = 0
    for packet, label_ref, start, count in (
        (train_packet, train_label, 0, train_count),
        (test_packet, test_label, train_count, test_count),
    ):
        own = pooled[pl.ds(start, count), :]
        logits = lax.dot_general(
            cls_rows[...],
            own,
            (((1,), (1,)), ((), ())),
            precision=lax.Precision.HIGHEST,
            preferred_element_type=jnp.float32,
        )
        labels = jnp.broadcast_to(label_ref[...].astype(jnp.float32), (NCLS, count))
        for target, first in ((packet, 0), (own_packet, at)):
            target[pl.ds(first, count), :] = own
            target[pl.ds(first + count, NCLS), pl.ds(0, count)] = logits
            target[pl.ds(first + count, NCLS), pl.ds(128, count)] = labels
        at += count + NCLS
    own_packet[pl.ds(at, seeds.shape[0]), pl.ds(0, 128)] = (seeds[...] >> 15).astype(jnp.float32)
    own_packet[pl.ds(at, seeds.shape[0]), pl.ds(128, 128)] = (seeds[...] & 32767).astype(jnp.float32)


def pool(train_windows, test_windows, weight, gain, cls_t, train_labels, test_labels, seeds):
    block = 16
    train_count, length, width = train_windows.shape
    test_count = test_windows.shape[0]
    half = weight.shape[2]
    total = train_count + test_count
    return pl.pallas_call(
        functools.partial(pool_kernel, block),
        out_shape=(
            jax.ShapeDtypeStruct((train_count + NCLS, half), jnp.float32),
            jax.ShapeDtypeStruct((test_count + NCLS, half), jnp.float32),
            jax.ShapeDtypeStruct((total + 2 * NCLS + seeds.shape[0], half), jnp.float32),
        ),
        in_specs=[HBM] * 8,
        out_specs=(VMEM, VMEM, VMEM),
        scratch_shapes=[
            pltpu.VMEM((total, length, width), jnp.bfloat16),
            pltpu.VMEM(weight.shape, jnp.bfloat16),
            pltpu.VMEM((total, half), jnp.float32),
            pltpu.VMEM(gain.shape, jnp.float32),
            pltpu.VMEM(cls_t.shape, jnp.float32),
            pltpu.VMEM(train_labels.shape, jnp.int32),
            pltpu.VMEM(test_labels.shape, jnp.int32),
            pltpu.VMEM(seeds.shape, jnp.int32),
            pltpu.SemaphoreType.DMA((total // block,)),
            pltpu.SemaphoreType.DMA,
            pltpu.SemaphoreType.DMA((5,)),
        ],
        compiler_params=pltpu.CompilerParams(vmem_limit_bytes=24 * MIB),
        name="pool",
    )(
        *(
            pltpu.with_memory_space_constraint(value, pltpu.HBM)
            for value in (train_windows, test_windows, weight, gain, cls_t, train_labels, test_labels, seeds)
        )
    )


def sign_kernel(packed, classes, seed_ref, sign_ref, turned, column_ref):
    proj_index = lax.axis_index("proj")
    parts, rows, part_width = sign_ref.shape
    count = parts * part_width
    chunks = rows // ((128 // NCLS) * len(classes))
    per_chunk = 128 // NCLS
    if packed:
        first = seed_ref.shape[0] - chunks
        high = seed_ref[pl.ds(first, chunks), pl.ds(0, 128)].astype(jnp.int32)
        seeds = high * 32768 + seed_ref[pl.ds(first, chunks), pl.ds(128, 128)].astype(jnp.int32)
    else:
        seeds = seed_ref[...]
    turned[:, pl.ds(0, chunks)] = seeds.T

    @pl.when(proj_index >= 0)
    def _():
        column_ref[...] = (
            lax.broadcasted_iota(jnp.int32, column_ref.shape, 1) + proj_index * count
        ) * MIX_COLUMN

    for k in classes:
        seeds = turned[pl.ds(k, per_chunk, stride=NCLS), :]
        for h in range(chunks):
            mixed = (seeds[:, h : h + 1] ^ column_ref[...]) * MIX_FIRST
            mixed = (mixed ^ (mixed >> 13)) * MIX_LAST
            signs = jnp.where(mixed < 0, -1.0, 1.0).astype(jnp.bfloat16)
            at = ((k - classes[0]) * chunks + h) * per_chunk
            for n in range(parts):
                sign_ref[n, pl.ds(at, per_chunk), :] = signs[:, n * part_width : (n + 1) * part_width]


def sign_block(seeds, channels, count, classes):
    rows = channels * len(classes)
    parts = count // 256
    return pl.pallas_call(
        functools.partial(sign_kernel, seeds.dtype == jnp.float32, classes),
        out_shape=jax.ShapeDtypeStruct((parts, rows, 256), jnp.bfloat16),
        in_specs=[VMEM],
        out_specs=VMEM,
        scratch_shapes=[pltpu.VMEM((128, 128), jnp.int32), pltpu.VMEM((128 // NCLS, count), jnp.int32)],
        compiler_params=pltpu.CompilerParams(vmem_limit_bytes=16 * MIB),
        cost_estimate=pl.CostEstimate(
            flops=8 * rows * count, bytes_accessed=2 * rows * count, transcendentals=0
        ),
        name="signs",
    )(seeds)


def score_kernel(train_blocks, test_blocks, train_count, test_count, *refs):
    far = train_blocks + test_blocks - 2
    packets = refs[: 2 * far + 2]
    signs = refs[2 * far + 2 : -5]
    precond_ref, keep_ref, send_ref, train_feat, test_feat = refs[-5:]
    proj_index = lax.axis_index("proj")
    parts, _, part_width = signs[0].shape
    train_rows = train_blocks * train_count
    gradients = []
    row_weights = []
    for i in range(train_blocks + test_blocks):
        first = 0
        if i == 0:
            mine, theirs = packets[0], packets[1]
        elif i < train_blocks:
            mine, theirs = packets[2 * i], packets[2 * i + 1]
        elif i == train_blocks:
            mine, theirs = packets[0], packets[1]
            first = train_count + NCLS
        else:
            mine, theirs = packets[2 * (i - 1)], packets[2 * (i - 1) + 1]
        count = train_count if i < train_blocks else test_count
        class_rows = pl.ds(first + count, NCLS)
        logits = mine[class_rows, pl.ds(0, 128)] + theirs[class_rows, pl.ds(0, 128)]
        label = mine[class_rows, pl.ds(128, 128)]
        chance = 1.0 / (1.0 + jnp.exp(-logits))
        classes = lax.broadcasted_iota(jnp.int32, (NCLS, 128), 0).astype(jnp.float32)
        target = jnp.where(label == classes, 1.0, 0.0)
        retain = 1.0 - jnp.sum(chance * target, axis=0, keepdims=True)
        stacked = jnp.concatenate([chance - target, jnp.broadcast_to(retain, (NCLS, 128))], axis=0)
        turned = stacked.T[:count]
        if i < train_blocks:
            row_weights.append(turned[:, NCLS : NCLS + 1])
        pieces = []
        for packet in (mine, theirs):
            value = packet[pl.ds(first, count), :]
            for k in range(NCLS):
                pieces.append((value * turned[:, k : k + 1]).astype(jnp.bfloat16))
        gradients.append(jnp.concatenate(pieces, axis=1))
    gradient = jnp.concatenate(gradients, axis=0)
    train_index, test_index = lax.axis_index("train"), lax.axis_index("test")
    for n in range(parts):
        projected = jnp.dot(
            gradient,
            jnp.concatenate([value[n] for value in signs], axis=0),
            preferred_element_type=jnp.float32,
        )
        columns = pl.ds(n * part_width, part_width)
        for i in range(train_blocks):
            part = projected[i * train_count : (i + 1) * train_count]
            train_feat[_source(train_index, i, train_blocks), :, columns] = (
                part * row_weights[i]
            ).astype(jnp.bfloat16)
        precond = precond_ref[
            :, pl.ds(pl.multiple_of(proj_index * (parts * part_width) + n * part_width, 128), part_width)
        ]
        for i in range(test_blocks):
            start = train_rows + i * test_count
            test_feat[_source(test_index, i, test_blocks), :, columns] = (
                projected[start : start + test_count] * precond
            ).astype(jnp.bfloat16)
    half_blocks = train_blocks // 2
    test = test_feat[...].reshape(test_blocks * test_count, parts * part_width)
    for target, side in ((send_ref, 1 - proj_index), (keep_ref, proj_index)):
        train = train_feat[pl.ds(side * half_blocks, half_blocks)].reshape(
            half_blocks * train_count, parts * part_width
        )
        target[...] = lax.dot_general(
            test, train, (((1,), (1,)), ((), ())), preferred_element_type=jnp.float32
        )


def _source(index, shift, count):
    if count & (count - 1) == 0:
        return index ^ shift
    return lax.rem(index + count - shift, count)


def _pairs(shift, count):
    if count & (count - 1) == 0:
        return [(i, i ^ shift) for i in range(count)]
    return [(i, (i + shift) % count) for i in range(count)]


def partial_scores(packets, signs, precond, train_blocks, test_blocks, train_count, test_count):
    parts, _, part_width = signs[0].shape
    rows = sum(value.shape[1] for value in signs)
    out_rows = test_blocks * test_count
    out_cols = train_blocks * train_count
    total_rows = out_rows + out_cols
    return pl.pallas_call(
        functools.partial(score_kernel, train_blocks, test_blocks, train_count, test_count),
        out_shape=(jax.ShapeDtypeStruct((out_rows, out_cols // 2), jnp.float32),) * 2,
        in_specs=[VMEM] * (len(packets) + len(signs) + 1),
        out_specs=(VMEM, VMEM),
        scratch_shapes=[
            pltpu.VMEM((train_blocks, train_count, parts * part_width), jnp.bfloat16),
            pltpu.VMEM((test_blocks, test_count, parts * part_width), jnp.bfloat16),
        ],
        compiler_params=pltpu.CompilerParams(vmem_limit_bytes=40 * MIB),
        cost_estimate=pl.CostEstimate(
            flops=2 * total_rows * rows * parts * part_width,
            bytes_accessed=2 * rows * parts * part_width,
            transcendentals=0,
        ),
        name="partial_scores",
    )(*packets, *signs, precond)


def shards(
    train_windows,
    test_windows,
    train_labels,
    test_labels,
    dilated_weight,
    branch_gain,
    cls_weight,
    sign_seeds,
    precond,
):
    train_count = train_windows.shape[0]
    test_count = test_windows.shape[0]
    train_blocks = lax.axis_size("train")
    test_blocks = lax.axis_size("test")
    count = K // lax.axis_size("proj")
    swap = [(0, 1), (1, 0)]
    seeds = sign_seeds.reshape(-1, 128)
    train_packet, test_packet, own_packet = pool(
        train_windows,
        test_windows,
        dilated_weight,
        branch_gain.reshape(1, -1),
        cls_weight.T,
        train_labels.reshape(1, -1),
        test_labels.reshape(1, -1),
        seeds,
    )
    far = [lax.ppermute(train_packet, "train", _pairs(shift, train_blocks)) for shift in range(1, train_blocks)]
    far += [lax.ppermute(test_packet, "test", _pairs(shift, test_blocks)) for shift in range(1, test_blocks)]
    other_packet = lax.ppermute(own_packet, "proj", swap)
    early = [i for i in range(len(far)) if i >= train_blocks - 1 or i == train_blocks - 2]
    late = [i for i in range(len(far)) if i not in early]
    channels = sign_seeds.shape[0] // NCLS
    classes = tuple(range(NCLS))
    own_signs = sign_block(seeds, channels, count, classes)
    far_other = [None] * len(far)
    *held, own_signs, other_packet = lax.optimization_barrier((*(far[i] for i in early), own_signs, other_packet))
    for i, value in zip(early, held):
        far[i] = value
        far_other[i] = lax.ppermute(value, "proj", swap)
    first_signs = sign_block(other_packet, channels, count, classes[: NCLS // 2])
    *held, first_signs = lax.optimization_barrier((*(far[i] for i in late), first_signs))
    for i, value in zip(late, held):
        far[i] = value
        far_other[i] = lax.ppermute(value, "proj", swap)
    last_signs = sign_block(other_packet, channels, count, classes[NCLS // 2 :])
    packets = [own_packet, other_packet]
    for value, other in zip(far, far_other):
        packets += [value, other]
    keep, send = partial_scores(
        packets,
        [own_signs, first_signs, last_signs],
        precond.reshape(1, -1),
        train_blocks,
        test_blocks,
        train_count,
        test_count,
    )
    received = lax.ppermute(send, "proj", swap)
    return (keep + received) * (1.0 / (K * math.sqrt(C)))


def solution(mesh):
    return jax.shard_map(
        shards,
        mesh=mesh,
        in_specs=(
            P(("grp", "test", "train"), None, None),
            P(("grp", "train", "test"), None, None),
            P(("grp", "test", "train")),
            P(("grp", "train", "test")),
            P(None, None, "proj"),
            P("proj"),
            P("proj", None),
            P("proj"),
            P(),
        ),
        out_specs=P(("grp", "train"), ("test", "proj")),
        check_vma=False,
    )
```

```python
import functools
import math

import jax
import jax.numpy as jnp
from jax import lax
from jax.experimental import pallas as pl
from jax.experimental.pallas import tpu as pltpu
from jax.sharding import PartitionSpec as P

C = 512
NCLS = 8
K = 2048
DILATION_STEP = 4
MIX_COLUMN = 668265261
MIX_FIRST = 625341585
MIX_LAST = (1274126177 << 15) & 0xFFFFFFFF
MIX_LAST = MIX_LAST - (1 << 32) if MIX_LAST >= 1 << 31 else MIX_LAST
MIB = 2**20
AHEAD = 3
EARLY_CLASSES = tuple(range(1))

VMEM = pl.BlockSpec(memory_space=pltpu.VMEM)
HBM = pl.BlockSpec(memory_space=pltpu.HBM)


def write_signs(classes, seeds, sign_ref, turned, column_ref):
    proj_index = lax.axis_index("proj")
    parts, rows, part_width = sign_ref.shape
    count = parts * part_width
    per_chunk = 128 // NCLS
    chunks = rows // (per_chunk * len(classes))
    turned[:, pl.ds(0, chunks)] = seeds.T

    @pl.when(proj_index >= 0)
    def _():
        column_ref[...] = (
            lax.broadcasted_iota(jnp.int32, column_ref.shape, 1) + proj_index * count
        ) * MIX_COLUMN

    for k in classes:
        class_seeds = turned[pl.ds(k, per_chunk, stride=NCLS), :]
        for h in range(chunks):
            mixed = (class_seeds[:, h : h + 1] ^ column_ref[...]) * MIX_FIRST
            mixed = (mixed ^ (mixed >> 13)) * MIX_LAST
            signs = jnp.where(mixed < 0, -1.0, 1.0).astype(jnp.bfloat16)
            at = ((k - classes[0]) * chunks + h) * per_chunk
            for n in range(parts):
                sign_ref[n, pl.ds(at, per_chunk), :] = signs[:, n * part_width : (n + 1) * part_width]


def power_of_two(exponent):
    return jnp.exp(exponent * math.log(2.0))


def encode_packet(packet, pooled, logits, labels):
    count = pooled.shape[0]
    largest = jnp.maximum(jnp.max(jnp.abs(pooled), axis=1, keepdims=True), 1e-30)
    exponent = jnp.floor(jnp.log(largest) * (1.0 / math.log(2.0)))
    factor = jnp.ceil(largest * power_of_two(-exponent) * 8192.0)
    step = factor * (power_of_two(exponent) * (1.0 / (8192.0 * 32767.0)))
    steps = jnp.clip(jnp.round(pooled * (1.0 / step)), -32767.0, 32767.0)
    packet[pl.ds(0, count), :] = steps.astype(jnp.int32).astype(jnp.int16)
    lane = lax.broadcasted_iota(jnp.int32, (count, 128), 1)
    turned = jnp.where(lane == 1, factor, jnp.where(lane == 2, exponent, 0.0)).T[:NCLS]
    logit_exponent = jnp.ceil(
        jnp.log(jnp.maximum(jnp.max(jnp.abs(logits), axis=0, keepdims=True), 1e-30)) * (1.0 / math.log(2.0))
    )
    scaled = logits * (power_of_two(-logit_exponent) * 8192.0)
    high = jnp.round(scaled)
    low = jnp.round((scaled - high) * 16384.0)
    row = lax.broadcasted_iota(jnp.int32, (NCLS, count), 0)
    facts = jnp.where(row == 0, labels, jnp.where(row == 3, logit_exponent, turned))
    blank = jnp.zeros((NCLS, 128 - count), jnp.float32)
    extra = jnp.concatenate(
        [
            jnp.concatenate([high, blank, facts, blank], axis=1),
            jnp.concatenate([low, blank, jnp.zeros((NCLS, 128), jnp.float32)], axis=1),
        ],
        axis=0,
    )
    packet[pl.ds(count, 2 * NCLS), :] = extra.astype(jnp.int32).astype(jnp.int16)


def decode_packet(packet):
    count = packet.shape[0] - 2 * NCLS
    steps = packet[pl.ds(0, count), :].astype(jnp.int32).astype(jnp.float32)
    extra = packet[pl.ds(count, 2 * NCLS), :].astype(jnp.int32).astype(jnp.float32)
    facts = extra[:NCLS, 128:]
    step = facts[1:2] * (power_of_two(facts[2:3]) * (1.0 / (8192.0 * 32767.0)))
    logits = (extra[:NCLS, :128] + extra[NCLS:, :128] * (1.0 / 16384.0)) * (
        power_of_two(facts[3:4]) * (1.0 / 8192.0)
    )
    return steps, step, logits, facts[0:1]


def pool_kernel(
    block,
    train_hbm,
    test_hbm,
    weight_hbm,
    gain_ref,
    cls_ref,
    train_label_ref,
    test_label_ref,
    seed_ref,
    train_packet,
    test_packet,
    own_packet,
    sign_ref,
    rows,
    weight,
    pooled,
    gain_row,
    cls_rows,
    train_label,
    test_label,
    seeds,
    turned,
    column_ref,
    row_sem,
    weight_sem,
    small_sem,
):
    proj_index = lax.axis_index("proj")
    train_count, length, width = train_hbm.shape
    test_count = test_hbm.shape[0]
    half = weight.shape[2]
    blocks = (train_count + test_count) // block
    small = [
        pltpu.make_async_copy(source, target, small_sem.at[i])
        for i, (source, target) in enumerate(
            (
                (gain_ref, gain_row),
                (cls_ref, cls_rows),
                (train_label_ref, train_label),
                (test_label_ref, test_label),
                (seed_ref, seeds),
            )
        )
    ]
    for copy in small:
        copy.start()
    weight_copy = pltpu.make_async_copy(weight_hbm, weight, weight_sem)
    weight_copy.start()

    def fetch(b):
        source = train_hbm if b < train_count // block else test_hbm
        offset = b * block if b < train_count // block else b * block - train_count
        return pltpu.make_async_copy(
            source.at[pl.ds(offset, block)], rows.at[pl.ds(b * block, block)], row_sem.at[b]
        )

    for b in range(min(AHEAD, blocks)):
        fetch(b).start()
    for copy in small:
        copy.wait()
    write_signs(EARLY_CLASSES, seeds[...], sign_ref, turned, column_ref)
    weight_copy.wait()
    gain = gain_row[...]
    own_start = pl.multiple_of(proj_index * half, half)

    def one_block(b, carry):
        start = b * block
        for late in range(AHEAD, blocks):

            @pl.when(b == late - AHEAD)
            def _():
                fetch(late).start()

        pltpu.make_async_copy(
            test_hbm.at[pl.ds(0, block)], rows.at[pl.ds(start, block)], row_sem.at[b]
        ).wait()
        x = rows[pl.ds(start, block)]
        zeros = jnp.zeros((block, DILATION_STEP, width), x.dtype)
        before = jnp.concatenate([zeros, x[:, : length - DILATION_STEP]], axis=1)
        after = jnp.concatenate([x[:, DILATION_STEP:], zeros], axis=1)
        taps = jnp.concatenate([before, x, after], axis=2).reshape(block * length, 3 * width)
        conv = jnp.dot(
            taps, weight[...].reshape(3 * width, half), preferred_element_type=jnp.float32
        ).reshape(block, length, half)
        own = rows[pl.ds(start, block), :, pl.ds(own_start, half)].astype(jnp.float32)
        total = jnp.sum(own, axis=1) + gain * jnp.sum(jnp.maximum(conv, 0.0), axis=1)
        pooled[pl.ds(pl.multiple_of(start, block), block), :] = total * (1.0 / length)
        return carry

    lax.fori_loop(0, blocks, one_block, 0)
    at = 0
    for packet, label_ref, start, count in (
        (train_packet, train_label, 0, train_count),
        (test_packet, test_label, train_count, test_count),
    ):
        own = pooled[pl.ds(start, count), :]
        logits = lax.dot_general(
            cls_rows[...],
            own,
            (((1,), (1,)), ((), ())),
            precision=lax.Precision.HIGHEST,
            preferred_element_type=jnp.float32,
        )
        labels = jnp.broadcast_to(label_ref[...].astype(jnp.float32), (NCLS, count))
        own_packet[pl.ds(at, count), :] = own
        own_packet[pl.ds(at + count, NCLS), pl.ds(0, count)] = logits
        own_packet[pl.ds(at + count, NCLS), pl.ds(128, count)] = labels
        encode_packet(packet, own, logits, labels)
        at += count + NCLS
    own_packet[pl.ds(at, seeds.shape[0]), pl.ds(0, 128)] = (seeds[...] >> 15).astype(jnp.float32)
    own_packet[pl.ds(at, seeds.shape[0]), pl.ds(128, 128)] = (seeds[...] & 32767).astype(jnp.float32)


def pool(train_windows, test_windows, weight, gain, cls_t, train_labels, test_labels, seeds, count):
    block = 16
    train_count, length, width = train_windows.shape
    test_count = test_windows.shape[0]
    half = weight.shape[2]
    total = train_count + test_count
    return pl.pallas_call(
        functools.partial(pool_kernel, block),
        out_shape=(
            jax.ShapeDtypeStruct((train_count + 2 * NCLS, half), jnp.int16),
            jax.ShapeDtypeStruct((test_count + 2 * NCLS, half), jnp.int16),
            jax.ShapeDtypeStruct((total + 2 * NCLS + seeds.shape[0], half), jnp.float32),
            jax.ShapeDtypeStruct((count // 256, seeds.size // NCLS * len(EARLY_CLASSES), 256), jnp.bfloat16),
        ),
        in_specs=[HBM] * 8,
        out_specs=(VMEM, VMEM, VMEM, VMEM),
        scratch_shapes=[
            pltpu.VMEM((total, length, width), jnp.bfloat16),
            pltpu.VMEM(weight.shape, jnp.bfloat16),
            pltpu.VMEM((total, half), jnp.float32),
            pltpu.VMEM(gain.shape, jnp.float32),
            pltpu.VMEM(cls_t.shape, jnp.float32),
            pltpu.VMEM(train_labels.shape, jnp.int32),
            pltpu.VMEM(test_labels.shape, jnp.int32),
            pltpu.VMEM(seeds.shape, jnp.int32),
            pltpu.VMEM((128, 128), jnp.int32),
            pltpu.VMEM((128 // NCLS, count), jnp.int32),
            pltpu.SemaphoreType.DMA((total // block,)),
            pltpu.SemaphoreType.DMA,
            pltpu.SemaphoreType.DMA((5,)),
        ],
        compiler_params=pltpu.CompilerParams(vmem_limit_bytes=24 * MIB),
        name="pool",
    )(
        *(
            pltpu.with_memory_space_constraint(value, pltpu.HBM)
            for value in (train_windows, test_windows, weight, gain, cls_t, train_labels, test_labels, seeds)
        )
    )


def sign_kernel(packed, classes, seed_ref, sign_ref, turned, column_ref):
    if packed:
        chunks = sign_ref.shape[1] // ((128 // NCLS) * len(classes))
        first = seed_ref.shape[0] - chunks
        high = seed_ref[pl.ds(first, chunks), pl.ds(0, 128)].astype(jnp.int32)
        seeds = high * 32768 + seed_ref[pl.ds(first, chunks), pl.ds(128, 128)].astype(jnp.int32)
    else:
        seeds = seed_ref[...]
    write_signs(classes, seeds, sign_ref, turned, column_ref)


def sign_block(seeds, channels, count, classes):
    rows = channels * len(classes)
    parts = count // 256
    return pl.pallas_call(
        functools.partial(sign_kernel, seeds.dtype == jnp.float32, classes),
        out_shape=jax.ShapeDtypeStruct((parts, rows, 256), jnp.bfloat16),
        in_specs=[VMEM],
        out_specs=VMEM,
        scratch_shapes=[pltpu.VMEM((128, 128), jnp.int32), pltpu.VMEM((128 // NCLS, count), jnp.int32)],
        compiler_params=pltpu.CompilerParams(vmem_limit_bytes=16 * MIB),
        cost_estimate=pl.CostEstimate(
            flops=8 * rows * count, bytes_accessed=2 * rows * count, transcendentals=0
        ),
        name="signs",
    )(seeds)


def score_kernel(train_blocks, test_blocks, train_count, test_count, *refs):
    far = train_blocks + test_blocks - 2
    packets = refs[: 2 * far + 2]
    signs = refs[2 * far + 2 : -5]
    precond_ref, keep_ref, send_ref, train_feat, test_feat = refs[-5:]
    proj_index = lax.axis_index("proj")
    parts, _, part_width = signs[0].shape
    train_rows = train_blocks * train_count
    gradients = []
    row_weights = []
    for i in range(train_blocks + test_blocks):
        count = train_count if i < train_blocks else test_count
        if i == 0 or i == train_blocks:
            first = 0 if i == 0 else train_count + NCLS
            values, logits, steps = [], 0.0, []
            for packet in packets[:2]:
                values.append(packet[pl.ds(first, count), :])
                logits += packet[pl.ds(first + count, NCLS), pl.ds(0, 128)]
            label = packets[0][pl.ds(first + count, 1), pl.ds(128, 128)]
        else:
            at = 2 * i if i < train_blocks else 2 * (i - 1)
            decoded = [decode_packet(packet) for packet in packets[at : at + 2]]
            values = [value for value, _, _, _ in decoded]
            steps = [step for _, step, _, _ in decoded]
            logits = decoded[0][2] + decoded[1][2]
            label = decoded[0][3]
        chance = 1.0 / (1.0 + jnp.exp(-logits))
        classes = lax.broadcasted_iota(jnp.int32, (NCLS, 128), 0).astype(jnp.float32)
        target = jnp.where(label == classes, 1.0, 0.0)
        retain = 1.0 - jnp.sum(chance * target, axis=0, keepdims=True)
        rest = [retain, *steps]
        rest += [jnp.zeros((NCLS - len(rest), 128), jnp.float32)]
        turned = jnp.concatenate([chance - target, *rest], axis=0).T[:count]
        if i < train_blocks:
            row_weights.append(turned[:, NCLS : NCLS + 1])
        pieces = []
        for value_index, value in enumerate(values):
            if steps:
                value = value * turned[:, NCLS + 1 + value_index : NCLS + 2 + value_index]
            for k in range(NCLS):
                pieces.append((value * turned[:, k : k + 1]).astype(jnp.bfloat16))
        gradients.append(jnp.concatenate(pieces, axis=1))
    gradient = jnp.concatenate(gradients, axis=0)
    train_index, test_index = lax.axis_index("train"), lax.axis_index("test")
    for n in range(parts):
        projected = jnp.dot(
            gradient,
            jnp.concatenate([value[n] for value in signs], axis=0),
            preferred_element_type=jnp.float32,
        )
        columns = pl.ds(n * part_width, part_width)
        for i in range(train_blocks):
            part = projected[i * train_count : (i + 1) * train_count]
            train_feat[_source(train_index, i, train_blocks), :, columns] = (
                part * row_weights[i]
            ).astype(jnp.bfloat16)
        precond = precond_ref[
            :, pl.ds(pl.multiple_of(proj_index * (parts * part_width) + n * part_width, 128), part_width)
        ]
        for i in range(test_blocks):
            start = train_rows + i * test_count
            test_feat[_source(test_index, i, test_blocks), :, columns] = (
                projected[start : start + test_count] * precond
            ).astype(jnp.bfloat16)
    half_blocks = train_blocks // 2
    test = test_feat[...].reshape(test_blocks * test_count, parts * part_width)
    for target, side in ((send_ref, 1 - proj_index), (keep_ref, proj_index)):
        train = train_feat[pl.ds(side * half_blocks, half_blocks)].reshape(
            half_blocks * train_count, parts * part_width
        )
        target[...] = lax.dot_general(
            test, train, (((1,), (1,)), ((), ())), preferred_element_type=jnp.float32
        )


def _source(index, shift, count):
    if count & (count - 1) == 0:
        return index ^ shift
    return lax.rem(index + count - shift, count)


def _pairs(shift, count):
    if count & (count - 1) == 0:
        return [(i, i ^ shift) for i in range(count)]
    return [(i, (i + shift) % count) for i in range(count)]


def partial_scores(packets, signs, precond, train_blocks, test_blocks, train_count, test_count):
    parts, _, part_width = signs[0].shape
    rows = sum(value.shape[1] for value in signs)
    out_rows = test_blocks * test_count
    out_cols = train_blocks * train_count
    total_rows = out_rows + out_cols
    return pl.pallas_call(
        functools.partial(score_kernel, train_blocks, test_blocks, train_count, test_count),
        out_shape=(jax.ShapeDtypeStruct((out_rows, out_cols // 2), jnp.float32),) * 2,
        in_specs=[VMEM] * (len(packets) + len(signs) + 1),
        out_specs=(VMEM, VMEM),
        scratch_shapes=[
            pltpu.VMEM((train_blocks, train_count, parts * part_width), jnp.bfloat16),
            pltpu.VMEM((test_blocks, test_count, parts * part_width), jnp.bfloat16),
        ],
        compiler_params=pltpu.CompilerParams(vmem_limit_bytes=40 * MIB),
        cost_estimate=pl.CostEstimate(
            flops=2 * total_rows * rows * parts * part_width,
            bytes_accessed=2 * rows * parts * part_width,
            transcendentals=0,
        ),
        name="partial_scores",
    )(*packets, *signs, precond)


def shards(
    train_windows,
    test_windows,
    train_labels,
    test_labels,
    dilated_weight,
    branch_gain,
    cls_weight,
    sign_seeds,
    precond,
):
    train_count = train_windows.shape[0]
    test_count = test_windows.shape[0]
    train_blocks = lax.axis_size("train")
    test_blocks = lax.axis_size("test")
    count = K // lax.axis_size("proj")
    swap = [(0, 1), (1, 0)]
    seeds = sign_seeds.reshape(-1, 128)
    train_packet, test_packet, own_packet, early_signs = pool(
        train_windows,
        test_windows,
        dilated_weight,
        branch_gain.reshape(1, -1),
        cls_weight.T,
        train_labels.reshape(1, -1),
        test_labels.reshape(1, -1),
        seeds,
        count,
    )
    far = [lax.ppermute(train_packet, "train", _pairs(shift, train_blocks)) for shift in range(1, train_blocks)]
    far += [lax.ppermute(test_packet, "test", _pairs(shift, test_blocks)) for shift in range(1, test_blocks)]
    other_packet = lax.ppermute(own_packet, "proj", swap)
    channels = sign_seeds.shape[0] // NCLS
    classes = tuple(range(NCLS))
    own_signs = sign_block(seeds, channels, count, classes[len(EARLY_CLASSES) :])
    first_signs = sign_block(other_packet, channels, count, classes[: NCLS // 2])
    *far, own_signs, first_signs = lax.optimization_barrier((*far, own_signs, first_signs))
    far_other = [lax.ppermute(value, "proj", swap) for value in far]
    last_signs = sign_block(other_packet, channels, count, classes[NCLS // 2 :])
    packets = [own_packet, other_packet]
    for value, other in zip(far, far_other):
        packets += [value, other]
    keep, send = partial_scores(
        packets,
        [early_signs, own_signs, first_signs, last_signs],
        precond.reshape(1, -1),
        train_blocks,
        test_blocks,
        train_count,
        test_count,
    )
    received = lax.ppermute(send, "proj", swap)
    return (keep + received) * (1.0 / (K * math.sqrt(C)))


def solution(mesh):
    return jax.shard_map(
        shards,
        mesh=mesh,
        in_specs=(
            P(("grp", "test", "train"), None, None),
            P(("grp", "train", "test"), None, None),
            P(("grp", "test", "train")),
            P(("grp", "train", "test")),
            P(None, None, "proj"),
            P("proj"),
            P("proj", None),
            P("proj"),
            P(),
        ),
        out_specs=P(("grp", "train"), ("test", "proj")),
        check_vma=False,
    )
```

```python
import functools
import math

import jax
import jax.numpy as jnp
from jax import lax
from jax.experimental import pallas as pl
from jax.experimental.pallas import tpu as pltpu
from jax.sharding import PartitionSpec as P

C = 512
NCLS = 8
K = 2048
DILATION_STEP = 4
MIX_COLUMN = 668265261
MIX_FIRST = 625341585
MIX_LAST = (1274126177 << 15) & 0xFFFFFFFF
MIX_LAST = MIX_LAST - (1 << 32) if MIX_LAST >= 1 << 31 else MIX_LAST
MIB = 2**20
AHEAD = 3

VMEM = pl.BlockSpec(memory_space=pltpu.VMEM)
HBM = pl.BlockSpec(memory_space=pltpu.HBM)


def write_signs(classes, seeds, sign_ref, turned, column_ref):
    proj_index = lax.axis_index("proj")
    parts, rows, part_width = sign_ref.shape
    count = parts * part_width
    per_chunk = 128 // NCLS
    chunks = rows // (per_chunk * len(classes))
    turned[:, pl.ds(0, chunks)] = seeds.T

    @pl.when(proj_index >= 0)
    def _():
        column_ref[...] = (
            lax.broadcasted_iota(jnp.int32, column_ref.shape, 1) + proj_index * count
        ) * MIX_COLUMN

    for k in classes:
        class_seeds = turned[pl.ds(k, per_chunk, stride=NCLS), :]
        for h in range(chunks):
            mixed = (class_seeds[:, h : h + 1] ^ column_ref[...]) * MIX_FIRST
            mixed = (mixed ^ (mixed >> 13)) * MIX_LAST
            signs = jnp.where(mixed < 0, -1.0, 1.0).astype(jnp.bfloat16)
            at = ((k - classes[0]) * chunks + h) * per_chunk
            for n in range(parts):
                sign_ref[n, pl.ds(at, per_chunk), :] = signs[:, n * part_width : (n + 1) * part_width]


def power_of_two(exponent):
    return jnp.exp(exponent * math.log(2.0))


def encode_packet(packet, at, pooled, logits, labels):
    count = pooled.shape[0]
    largest = jnp.maximum(jnp.max(jnp.abs(pooled), axis=1, keepdims=True), 1e-30)
    exponent = jnp.floor(jnp.log(largest) * (1.0 / math.log(2.0)))
    factor = jnp.ceil(largest * power_of_two(-exponent) * 8192.0)
    step = factor * (power_of_two(exponent) * (1.0 / (8192.0 * 32767.0)))
    steps = jnp.clip(jnp.round(pooled * (1.0 / step)), -32767.0, 32767.0)
    packet[pl.ds(at, count), :] = steps.astype(jnp.int32).astype(jnp.int16)
    lane = lax.broadcasted_iota(jnp.int32, (count, 128), 1)
    turned = jnp.where(lane == 1, factor, jnp.where(lane == 2, exponent, 0.0)).T[:NCLS]
    logit_exponent = jnp.ceil(
        jnp.log(jnp.maximum(jnp.max(jnp.abs(logits), axis=0, keepdims=True), 1e-30)) * (1.0 / math.log(2.0))
    )
    scaled = logits * (power_of_two(-logit_exponent) * 8192.0)
    high = jnp.round(scaled)
    low = jnp.round((scaled - high) * 16384.0)
    row = lax.broadcasted_iota(jnp.int32, (NCLS, count), 0)
    facts = jnp.where(row == 0, labels, jnp.where(row == 3, logit_exponent, turned))
    blank = jnp.zeros((NCLS, 128 - count), jnp.float32)
    extra = jnp.concatenate(
        [
            jnp.concatenate([high, blank, facts, blank], axis=1),
            jnp.concatenate([low, blank, jnp.zeros((NCLS, 128), jnp.float32)], axis=1),
        ],
        axis=0,
    )
    packet[pl.ds(at + count, 2 * NCLS), :] = extra.astype(jnp.int32).astype(jnp.int16)


def decode_packet(packet):
    count = packet.shape[0] - 2 * NCLS
    extra = packet[count:]
    facts = extra[:NCLS, 128:]
    step = facts[1:2] * (power_of_two(facts[2:3]) * (1.0 / (8192.0 * 32767.0)))
    logits = (extra[:NCLS, :128] + extra[NCLS:, :128] * (1.0 / 16384.0)) * (
        power_of_two(facts[3:4]) * (1.0 / 8192.0)
    )
    return packet[:count], step, logits, facts[0:1]


def as_float(values):
    return values.astype(jnp.int32).astype(jnp.float32)


def pool_kernel(
    block,
    train_hbm,
    test_hbm,
    weight_hbm,
    gain_ref,
    cls_ref,
    train_label_ref,
    test_label_ref,
    seed_ref,
    packet,
    rows,
    weight,
    pooled,
    gain_row,
    cls_rows,
    train_label,
    test_label,
    seeds,
    row_sem,
    weight_sem,
    small_sem,
):
    proj_index = lax.axis_index("proj")
    train_count, length, width = train_hbm.shape
    test_count = test_hbm.shape[0]
    half = weight.shape[2]
    blocks = (train_count + test_count) // block
    small = [
        pltpu.make_async_copy(source, target, small_sem.at[i])
        for i, (source, target) in enumerate(
            (
                (gain_ref, gain_row),
                (cls_ref, cls_rows),
                (train_label_ref, train_label),
                (test_label_ref, test_label),
                (seed_ref, seeds),
            )
        )
    ]
    for copy in small:
        copy.start()
    weight_copy = pltpu.make_async_copy(weight_hbm, weight, weight_sem)
    weight_copy.start()

    def fetch(b):
        source = train_hbm if b < train_count // block else test_hbm
        offset = b * block if b < train_count // block else b * block - train_count
        return pltpu.make_async_copy(
            source.at[pl.ds(offset, block)], rows.at[pl.ds(b * block, block)], row_sem.at[b]
        )

    for b in range(min(AHEAD, blocks)):
        fetch(b).start()
    for copy in small:
        copy.wait()
    weight_copy.wait()
    gain = gain_row[...]
    own_start = pl.multiple_of(proj_index * half, half)

    def one_block(b, carry):
        start = b * block
        for late in range(AHEAD, blocks):

            @pl.when(b == late - AHEAD)
            def _():
                fetch(late).start()

        pltpu.make_async_copy(
            test_hbm.at[pl.ds(0, block)], rows.at[pl.ds(start, block)], row_sem.at[b]
        ).wait()
        x = rows[pl.ds(start, block)]
        zeros = jnp.zeros((block, DILATION_STEP, width), x.dtype)
        before = jnp.concatenate([zeros, x[:, : length - DILATION_STEP]], axis=1)
        after = jnp.concatenate([x[:, DILATION_STEP:], zeros], axis=1)
        taps = jnp.concatenate([before, x, after], axis=2).reshape(block * length, 3 * width)
        conv = jnp.dot(
            taps, weight[...].reshape(3 * width, half), preferred_element_type=jnp.float32
        ).reshape(block, length, half)
        own = rows[pl.ds(start, block), :, pl.ds(own_start, half)].astype(jnp.float32)
        total = jnp.sum(own, axis=1) + gain * jnp.sum(jnp.maximum(conv, 0.0), axis=1)
        pooled[pl.ds(pl.multiple_of(start, block), block), :] = total * (1.0 / length)
        return carry

    lax.fori_loop(0, blocks, one_block, 0)
    at = 0
    for label_ref, start, count in ((train_label, 0, train_count), (test_label, train_count, test_count)):
        own = pooled[pl.ds(start, count), :]
        logits = lax.dot_general(
            cls_rows[...],
            own,
            (((1,), (1,)), ((), ())),
            precision=lax.Precision.HIGHEST,
            preferred_element_type=jnp.float32,
        )
        labels = jnp.broadcast_to(label_ref[...].astype(jnp.float32), (NCLS, count))
        encode_packet(packet, at, own, logits, labels)
        at += count + 2 * NCLS
    packet[pl.ds(at, seeds.shape[0]), pl.ds(0, 128)] = (seeds[...] >> 15).astype(jnp.int16)
    packet[pl.ds(at, seeds.shape[0]), pl.ds(128, 128)] = (seeds[...] & 32767).astype(jnp.int16)


def pool(train_windows, test_windows, weight, gain, cls_t, train_labels, test_labels, seeds):
    block = 16
    train_count, length, width = train_windows.shape
    test_count = test_windows.shape[0]
    half = weight.shape[2]
    total = train_count + test_count
    return pl.pallas_call(
        functools.partial(pool_kernel, block),
        out_shape=jax.ShapeDtypeStruct((total + 4 * NCLS + seeds.shape[0], half), jnp.int16),
        in_specs=[HBM] * 8,
        out_specs=VMEM,
        scratch_shapes=[
            pltpu.VMEM((total, length, width), jnp.bfloat16),
            pltpu.VMEM(weight.shape, jnp.bfloat16),
            pltpu.VMEM((total, half), jnp.float32),
            pltpu.VMEM(gain.shape, jnp.float32),
            pltpu.VMEM(cls_t.shape, jnp.float32),
            pltpu.VMEM(train_labels.shape, jnp.int32),
            pltpu.VMEM(test_labels.shape, jnp.int32),
            pltpu.VMEM(seeds.shape, jnp.int32),
            pltpu.SemaphoreType.DMA((total // block,)),
            pltpu.SemaphoreType.DMA,
            pltpu.SemaphoreType.DMA((5,)),
        ],
        compiler_params=pltpu.CompilerParams(vmem_limit_bytes=24 * MIB),
        name="pool",
    )(
        *(
            pltpu.with_memory_space_constraint(value, pltpu.HBM)
            for value in (train_windows, test_windows, weight, gain, cls_t, train_labels, test_labels, seeds)
        )
    )


def transfer_steps(train_blocks, test_blocks):
    shifts = [("train", d) for d in reversed(range(1, train_blocks))]
    shifts += [("test", d) for d in range(1, test_blocks)]
    return [(shifts[i], shifts[i + 1]) for i in range(0, len(shifts), 2)]


def pack_kernel(kinds, train_rows, test_rows, mine, theirs, *outs):
    proj_index = lax.axis_index("proj")
    for pair, out in zip(kinds, outs):
        for core, kind in enumerate(pair):

            @pl.when(proj_index == core)
            def _():
                start, count = (0, train_rows) if kind == "train" else (train_rows, test_rows)
                for side, packet in enumerate((mine, theirs)):
                    out[side, pl.ds(0, count), :] = packet[pl.ds(start, count), :]


def pack(kinds, train_rows, test_rows, mine, theirs):
    width = mine.shape[1]
    rows = [train_rows if "train" in pair else test_rows for pair in kinds]
    return pl.pallas_call(
        functools.partial(pack_kernel, kinds, train_rows, test_rows),
        out_shape=tuple(jax.ShapeDtypeStruct((2, count, width), jnp.int16) for count in rows),
        in_specs=[VMEM, VMEM],
        out_specs=(VMEM,) * len(kinds),
        compiler_params=pltpu.CompilerParams(vmem_limit_bytes=8 * MIB),
        name="pack",
    )(mine, theirs)


def sign_kernel(packed, classes, seed_ref, sign_ref, turned, column_ref):
    if packed:
        chunks = sign_ref.shape[1] // ((128 // NCLS) * len(classes))
        first = seed_ref.shape[0] - chunks
        high = seed_ref[pl.ds(first, chunks), pl.ds(0, 128)].astype(jnp.int32)
        seeds = high * 32768 + seed_ref[pl.ds(first, chunks), pl.ds(128, 128)].astype(jnp.int32)
    else:
        seeds = seed_ref[...]
    write_signs(classes, seeds, sign_ref, turned, column_ref)


def sign_block(seeds, channels, count, classes):
    rows = channels * len(classes)
    parts = count // 256
    return pl.pallas_call(
        functools.partial(sign_kernel, seeds.dtype == jnp.int16, classes),
        out_shape=jax.ShapeDtypeStruct((parts, rows, 256), jnp.bfloat16),
        in_specs=[VMEM],
        out_specs=VMEM,
        scratch_shapes=[pltpu.VMEM((128, 128), jnp.int32), pltpu.VMEM((128 // NCLS, count), jnp.int32)],
        compiler_params=pltpu.CompilerParams(vmem_limit_bytes=16 * MIB),
        cost_estimate=pl.CostEstimate(
            flops=8 * rows * count, bytes_accessed=2 * rows * count, transcendentals=0
        ),
        name="signs",
    )(seeds)


def score_kernel(train_blocks, test_blocks, train_count, test_count, *refs):
    steps = transfer_steps(train_blocks, test_blocks)
    packets = refs[: 2 * len(steps) + 2]
    signs = refs[2 * len(steps) + 2 : -5]
    precond_ref, keep_ref, send_ref, train_feat, test_feat = refs[-5:]
    proj_index = lax.axis_index("proj")
    parts, _, part_width = signs[0].shape
    train_rows = train_blocks * train_count
    blocks = {"train": [], "test": []}
    for kind, first, count in (
        ("train", 0, train_count),
        ("test", train_count + 2 * NCLS, test_count),
    ):
        rows = pl.ds(first, count + 2 * NCLS)
        blocks[kind].append((0, [as_float(packet[rows, :]) for packet in packets[:2]]))
    for i, pair in enumerate(steps):
        direct, swapped = packets[2 * i + 2], packets[2 * i + 3]
        for core, (kind, shift) in enumerate(pair):
            rows = pl.ds(0, (train_count if kind == "train" else test_count) + 2 * NCLS)
            blocks[kind].append(
                (
                    shift,
                    [
                        jnp.where(
                            proj_index == core,
                            as_float(direct[side, rows, :]),
                            as_float(swapped[1 - side, rows, :]),
                        )
                        for side in range(2)
                    ],
                )
            )
    gradients = []
    row_weights = []
    for i, (_, pair) in enumerate(blocks["train"] + blocks["test"]):
        count = train_count if i < train_blocks else test_count
        decoded = [decode_packet(packet) for packet in pair]
        values = [value for value, _, _, _ in decoded]
        sizes = [step for _, step, _, _ in decoded]
        logits = decoded[0][2] + decoded[1][2]
        label = decoded[0][3]
        chance = 1.0 / (1.0 + jnp.exp(-logits))
        classes = lax.broadcasted_iota(jnp.int32, (NCLS, 128), 0).astype(jnp.float32)
        target = jnp.where(label == classes, 1.0, 0.0)
        retain = 1.0 - jnp.sum(chance * target, axis=0, keepdims=True)
        rest = [retain, *sizes]
        rest += [jnp.zeros((NCLS - len(rest), 128), jnp.float32)]
        turned = jnp.concatenate([chance - target, *rest], axis=0).T[:count]
        if i < train_blocks:
            row_weights.append(turned[:, NCLS : NCLS + 1])
        pieces = []
        for value_index, value in enumerate(values):
            value = value * turned[:, NCLS + 1 + value_index : NCLS + 2 + value_index]
            for k in range(NCLS):
                pieces.append((value * turned[:, k : k + 1]).astype(jnp.bfloat16))
        gradients.append(jnp.concatenate(pieces, axis=1))
    gradient = jnp.concatenate(gradients, axis=0)
    train_index, test_index = lax.axis_index("train"), lax.axis_index("test")
    for n in range(parts):
        projected = jnp.dot(
            gradient,
            jnp.concatenate([value[n] for value in signs], axis=0),
            preferred_element_type=jnp.float32,
        )
        columns = pl.ds(n * part_width, part_width)
        for i in range(train_blocks):
            part = projected[i * train_count : (i + 1) * train_count]
            train_feat[train_index ^ blocks["train"][i][0], :, columns] = (
                part * row_weights[i]
            ).astype(jnp.bfloat16)
        precond = precond_ref[
            :, pl.ds(pl.multiple_of(proj_index * (parts * part_width) + n * part_width, 128), part_width)
        ]
        for i in range(test_blocks):
            start = train_rows + i * test_count
            test_feat[test_index ^ blocks["test"][i][0], :, columns] = (
                projected[start : start + test_count] * precond
            ).astype(jnp.bfloat16)
    half_blocks = train_blocks // 2
    test = test_feat[...].reshape(test_blocks * test_count, parts * part_width)
    for target, side in ((send_ref, 1 - proj_index), (keep_ref, proj_index)):
        train = train_feat[pl.ds(side * half_blocks, half_blocks)].reshape(
            half_blocks * train_count, parts * part_width
        )
        target[...] = lax.dot_general(
            test, train, (((1,), (1,)), ((), ())), preferred_element_type=jnp.float32
        )


def partial_scores(packets, signs, precond, train_blocks, test_blocks, train_count, test_count):
    parts, _, part_width = signs[0].shape
    rows = sum(value.shape[1] for value in signs)
    out_rows = test_blocks * test_count
    out_cols = train_blocks * train_count
    total_rows = out_rows + out_cols
    return pl.pallas_call(
        functools.partial(score_kernel, train_blocks, test_blocks, train_count, test_count),
        out_shape=(jax.ShapeDtypeStruct((out_rows, out_cols // 2), jnp.float32),) * 2,
        in_specs=[VMEM] * (len(packets) + len(signs) + 1),
        out_specs=(VMEM, VMEM),
        scratch_shapes=[
            pltpu.VMEM((train_blocks, train_count, parts * part_width), jnp.bfloat16),
            pltpu.VMEM((test_blocks, test_count, parts * part_width), jnp.bfloat16),
        ],
        compiler_params=pltpu.CompilerParams(vmem_limit_bytes=40 * MIB),
        cost_estimate=pl.CostEstimate(
            flops=2 * total_rows * rows * parts * part_width,
            bytes_accessed=2 * rows * parts * part_width,
            transcendentals=0,
        ),
        name="partial_scores",
    )(*packets, *signs, precond)


def shards(
    train_windows,
    test_windows,
    train_labels,
    test_labels,
    dilated_weight,
    branch_gain,
    cls_weight,
    sign_seeds,
    precond,
):
    train_count = train_windows.shape[0]
    test_count = test_windows.shape[0]
    train_blocks = lax.axis_size("train")
    test_blocks = lax.axis_size("test")
    count = K // lax.axis_size("proj")
    swap = [(0, 1), (1, 0)]
    seeds = sign_seeds.reshape(-1, 128)
    packet = pool(
        train_windows,
        test_windows,
        dilated_weight,
        branch_gain.reshape(1, -1),
        cls_weight.T,
        train_labels.reshape(1, -1),
        test_labels.reshape(1, -1),
        seeds,
    )
    channels = sign_seeds.shape[0] // NCLS
    halves = (tuple(range(NCLS // 2)), tuple(range(NCLS // 2, NCLS)))
    steps = transfer_steps(train_blocks, test_blocks)
    other_packet = lax.ppermute(packet, "proj", swap)
    signs = [sign_block(seeds, channels, count, halves[0])]
    other_packet, signs[0] = lax.optimization_barrier((other_packet, signs[0]))
    kinds = list(dict.fromkeys((a, b) for (a, _), (b, _) in steps))
    packed = pack(kinds, train_count + 2 * NCLS, test_count + 2 * NCLS, packet, other_packet)
    far = []
    for pair in steps:
        moves = []
        for source in range(train_blocks * test_blocks * 2):
            core = source % 2
            kind, shift = pair[core]
            scale = 2 * test_blocks if kind == "train" else 2
            moves.append((source, source ^ (shift * scale)))
        value = packed[kinds.index((pair[0][0], pair[1][0]))]
        far.append(lax.ppermute(value, ("train", "test", "proj"), moves))
    signs.append(sign_block(seeds, channels, count, halves[1]))
    signs.append(sign_block(other_packet, channels, count, halves[0]))
    *far, signs[1], signs[2] = lax.optimization_barrier((*far, signs[1], signs[2]))
    packets = [packet, other_packet]
    for value in far:
        packets += [value, lax.ppermute(value, "proj", swap)]
    signs.append(sign_block(other_packet, channels, count, halves[1]))
    keep, send = partial_scores(
        packets, signs, precond.reshape(1, -1), train_blocks, test_blocks, train_count, test_count
    )
    received = lax.ppermute(send, "proj", swap)
    return (keep + received) * (1.0 / (K * math.sqrt(C)))


def solution(mesh):
    return jax.shard_map(
        shards,
        mesh=mesh,
        in_specs=(
            P(("grp", "test", "train"), None, None),
            P(("grp", "train", "test"), None, None),
            P(("grp", "test", "train")),
            P(("grp", "train", "test")),
            P(None, None, "proj"),
            P("proj"),
            P("proj", None),
            P("proj"),
            P(),
        ),
        out_specs=P(("grp", "train"), ("test", "proj")),
        check_vma=False,
    )
```

```python
import functools
import math

import jax
import jax.numpy as jnp
from jax import lax
from jax.experimental import pallas as pl
from jax.experimental.pallas import tpu as pltpu
from jax.sharding import PartitionSpec as P

C = 512
NCLS = 8
K = 2048
DILATION_STEP = 4
MIX_COLUMN = 668265261
MIX_FIRST = 625341585
MIX_LAST = (1274126177 << 15) & 0xFFFFFFFF
MIX_LAST = MIX_LAST - (1 << 32) if MIX_LAST >= 1 << 31 else MIX_LAST
MIB = 2**20
AHEAD = 3

VMEM = pl.BlockSpec(memory_space=pltpu.VMEM)
HBM = pl.BlockSpec(memory_space=pltpu.HBM)


def write_signs(classes, seeds, sign_ref, turned, column_ref):
    proj_index = lax.axis_index("proj")
    parts, rows, part_width = sign_ref.shape
    count = parts * part_width
    per_chunk = 128 // NCLS
    chunks = rows // (per_chunk * len(classes))
    turned[:, pl.ds(0, chunks)] = seeds.T

    @pl.when(proj_index >= 0)
    def _():
        column_ref[...] = (
            lax.broadcasted_iota(jnp.int32, column_ref.shape, 1) + proj_index * count
        ) * MIX_COLUMN

    for k in classes:
        class_seeds = turned[pl.ds(k, per_chunk, stride=NCLS), :]
        for h in range(chunks):
            mixed = (class_seeds[:, h : h + 1] ^ column_ref[...]) * MIX_FIRST
            mixed = (mixed ^ (mixed >> 13)) * MIX_LAST
            signs = jnp.where(mixed < 0, -1.0, 1.0).astype(jnp.bfloat16)
            at = ((k - classes[0]) * chunks + h) * per_chunk
            for n in range(parts):
                sign_ref[n, pl.ds(at, per_chunk), :] = signs[:, n * part_width : (n + 1) * part_width]


def power_of_two(exponent):
    return jnp.exp(exponent * math.log(2.0))


def encode_packet(packet, at, pooled, logits, labels):
    count = pooled.shape[0]
    largest = jnp.maximum(jnp.max(jnp.abs(pooled), axis=1, keepdims=True), 1e-30)
    exponent = jnp.floor(jnp.log(largest) * (1.0 / math.log(2.0)))
    factor = jnp.ceil(largest * power_of_two(-exponent) * 8192.0)
    step = factor * (power_of_two(exponent) * (1.0 / (8192.0 * 32767.0)))
    steps = jnp.clip(jnp.round(pooled * (1.0 / step)), -32767.0, 32767.0)
    packet[pl.ds(at, count), :] = steps.astype(jnp.int32).astype(jnp.int16)
    lane = lax.broadcasted_iota(jnp.int32, (count, 128), 1)
    turned = jnp.where(lane == 1, factor, jnp.where(lane == 2, exponent, 0.0)).T[:NCLS]
    logit_exponent = jnp.ceil(
        jnp.log(jnp.maximum(jnp.max(jnp.abs(logits), axis=0, keepdims=True), 1e-30)) * (1.0 / math.log(2.0))
    )
    scaled = logits * (power_of_two(-logit_exponent) * 8192.0)
    high = jnp.round(scaled)
    low = jnp.round((scaled - high) * 16384.0)
    row = lax.broadcasted_iota(jnp.int32, (NCLS, count), 0)
    facts = jnp.where(row == 0, labels, jnp.where(row == 3, logit_exponent, turned))
    blank = jnp.zeros((NCLS, 128 - count), jnp.float32)
    extra = jnp.concatenate(
        [
            jnp.concatenate([high, blank, facts, blank], axis=1),
            jnp.concatenate([low, blank, jnp.zeros((NCLS, 128), jnp.float32)], axis=1),
        ],
        axis=0,
    )
    packet[pl.ds(at + count, 2 * NCLS), :] = extra.astype(jnp.int32).astype(jnp.int16)


def decode_packet(packet):
    count = packet.shape[0] - 2 * NCLS
    extra = packet[count:]
    facts = extra[:NCLS, 128:]
    step = facts[1:2] * (power_of_two(facts[2:3]) * (1.0 / (8192.0 * 32767.0)))
    logits = (extra[:NCLS, :128] + extra[NCLS:, :128] * (1.0 / 16384.0)) * (
        power_of_two(facts[3:4]) * (1.0 / 8192.0)
    )
    return packet[:count], step, logits, facts[0:1]


def as_float(values):
    return values.astype(jnp.int32).astype(jnp.float32)


def pool_kernel(
    block,
    train_hbm,
    test_hbm,
    weight_hbm,
    gain_ref,
    cls_ref,
    train_label_ref,
    test_label_ref,
    seed_ref,
    packet,
    rows,
    weight,
    pooled,
    gain_row,
    cls_rows,
    train_label,
    test_label,
    seeds,
    row_sem,
    weight_sem,
    small_sem,
):
    proj_index = lax.axis_index("proj")
    train_count, length, width = train_hbm.shape
    test_count = test_hbm.shape[0]
    half = weight.shape[2]
    blocks = (train_count + test_count) // block
    small = [
        pltpu.make_async_copy(source, target, small_sem.at[i])
        for i, (source, target) in enumerate(
            (
                (gain_ref, gain_row),
                (cls_ref, cls_rows),
                (train_label_ref, train_label),
                (test_label_ref, test_label),
                (seed_ref, seeds),
            )
        )
    ]
    for copy in small:
        copy.start()
    weight_copy = pltpu.make_async_copy(weight_hbm, weight, weight_sem)
    weight_copy.start()

    def fetch(b):
        source = train_hbm if b < train_count // block else test_hbm
        offset = b * block if b < train_count // block else b * block - train_count
        return pltpu.make_async_copy(
            source.at[pl.ds(offset, block)], rows.at[pl.ds(b * block, block)], row_sem.at[b]
        )

    for b in range(min(AHEAD, blocks)):
        fetch(b).start()
    for copy in small:
        copy.wait()
    weight_copy.wait()
    gain = gain_row[...]
    own_start = pl.multiple_of(proj_index * half, half)

    def one_block(b, carry):
        start = b * block
        for late in range(AHEAD, blocks):

            @pl.when(b == late - AHEAD)
            def _():
                fetch(late).start()

        pltpu.make_async_copy(
            test_hbm.at[pl.ds(0, block)], rows.at[pl.ds(start, block)], row_sem.at[b]
        ).wait()
        x = rows[pl.ds(start, block)]
        zeros = jnp.zeros((block, DILATION_STEP, width), x.dtype)
        before = jnp.concatenate([zeros, x[:, : length - DILATION_STEP]], axis=1)
        after = jnp.concatenate([x[:, DILATION_STEP:], zeros], axis=1)
        taps = jnp.concatenate([before, x, after], axis=2).reshape(block * length, 3 * width)
        conv = jnp.dot(
            taps, weight[...].reshape(3 * width, half), preferred_element_type=jnp.float32
        ).reshape(block, length, half)
        own = rows[pl.ds(start, block), :, pl.ds(own_start, half)].astype(jnp.float32)
        total = jnp.sum(own, axis=1) + gain * jnp.sum(jnp.maximum(conv, 0.0), axis=1)
        pooled[pl.ds(pl.multiple_of(start, block), block), :] = total * (1.0 / length)
        return carry

    lax.fori_loop(0, blocks, one_block, 0)
    at = 0
    for label_ref, start, count in ((train_label, 0, train_count), (test_label, train_count, test_count)):
        own = pooled[pl.ds(start, count), :]
        logits = lax.dot_general(
            cls_rows[...],
            own,
            (((1,), (1,)), ((), ())),
            precision=lax.Precision.HIGHEST,
            preferred_element_type=jnp.float32,
        )
        labels = jnp.broadcast_to(label_ref[...].astype(jnp.float32), (NCLS, count))
        encode_packet(packet, at, own, logits, labels)
        at += count + 2 * NCLS
    packet[pl.ds(at, seeds.shape[0]), pl.ds(0, 128)] = (seeds[...] >> 15).astype(jnp.int16)
    packet[pl.ds(at, seeds.shape[0]), pl.ds(128, 128)] = (seeds[...] & 32767).astype(jnp.int16)


def pool(train_windows, test_windows, weight, gain, cls_t, train_labels, test_labels, seeds):
    block = 16
    train_count, length, width = train_windows.shape
    test_count = test_windows.shape[0]
    half = weight.shape[2]
    total = train_count + test_count
    return pl.pallas_call(
        functools.partial(pool_kernel, block),
        out_shape=jax.ShapeDtypeStruct((total + 4 * NCLS + seeds.shape[0], half), jnp.int16),
        in_specs=[HBM] * 8,
        out_specs=VMEM,
        scratch_shapes=[
            pltpu.VMEM((total, length, width), jnp.bfloat16),
            pltpu.VMEM(weight.shape, jnp.bfloat16),
            pltpu.VMEM((total, half), jnp.float32),
            pltpu.VMEM(gain.shape, jnp.float32),
            pltpu.VMEM(cls_t.shape, jnp.float32),
            pltpu.VMEM(train_labels.shape, jnp.int32),
            pltpu.VMEM(test_labels.shape, jnp.int32),
            pltpu.VMEM(seeds.shape, jnp.int32),
            pltpu.SemaphoreType.DMA((total // block,)),
            pltpu.SemaphoreType.DMA,
            pltpu.SemaphoreType.DMA((5,)),
        ],
        compiler_params=pltpu.CompilerParams(vmem_limit_bytes=24 * MIB),
        name="pool",
    )(
        *(
            pltpu.with_memory_space_constraint(value, pltpu.HBM)
            for value in (train_windows, test_windows, weight, gain, cls_t, train_labels, test_labels, seeds)
        )
    )


def transfer_steps(train_blocks, test_blocks):
    shifts = [("train", d) for d in reversed(range(1, train_blocks))]
    shifts += [("test", d) for d in range(1, test_blocks)]
    return [(shifts[i + 1], shifts[i]) for i in range(0, len(shifts), 2)]


def pack_kernel(kinds, train_rows, test_rows, mine, theirs, *outs):
    proj_index = lax.axis_index("proj")
    for pair, out in zip(kinds, outs):
        for core, kind in enumerate(pair):

            @pl.when(proj_index == core)
            def _():
                start, count = (0, train_rows) if kind == "train" else (train_rows, test_rows)
                for side, packet in enumerate((mine, theirs)):
                    out[side, pl.ds(0, count), :] = packet[pl.ds(start, count), :]


def pack(kinds, train_rows, test_rows, mine, theirs):
    width = mine.shape[1]
    rows = [train_rows if "train" in pair else test_rows for pair in kinds]
    return pl.pallas_call(
        functools.partial(pack_kernel, kinds, train_rows, test_rows),
        out_shape=tuple(jax.ShapeDtypeStruct((2, count, width), jnp.int16) for count in rows),
        in_specs=[VMEM, VMEM],
        out_specs=(VMEM,) * len(kinds),
        compiler_params=pltpu.CompilerParams(vmem_limit_bytes=8 * MIB),
        name="pack",
    )(mine, theirs)


def join_kernel(*refs):
    *values, out = refs
    at = 0
    for value in values:
        for side in range(value.shape[0]):
            out[pl.ds(at, value.shape[1]), :] = value[side]
            at += value.shape[1]


def join(values):
    rows = sum(value.shape[0] * value.shape[1] for value in values)
    return pl.pallas_call(
        join_kernel,
        out_shape=jax.ShapeDtypeStruct((rows, values[0].shape[2]), values[0].dtype),
        in_specs=[VMEM] * len(values),
        out_specs=VMEM,
        compiler_params=pltpu.CompilerParams(vmem_limit_bytes=8 * MIB),
        name="join",
    )(*values)


def sign_kernel(packed, classes, seed_ref, sign_ref, turned, column_ref):
    if packed:
        chunks = sign_ref.shape[1] // ((128 // NCLS) * len(classes))
        first = seed_ref.shape[0] - chunks
        high = seed_ref[pl.ds(first, chunks), pl.ds(0, 128)].astype(jnp.int32)
        seeds = high * 32768 + seed_ref[pl.ds(first, chunks), pl.ds(128, 128)].astype(jnp.int32)
    else:
        seeds = seed_ref[...]
    write_signs(classes, seeds, sign_ref, turned, column_ref)


def sign_block(seeds, channels, count, classes):
    rows = channels * len(classes)
    parts = count // 256
    return pl.pallas_call(
        functools.partial(sign_kernel, seeds.dtype == jnp.int16, classes),
        out_shape=jax.ShapeDtypeStruct((parts, rows, 256), jnp.bfloat16),
        in_specs=[VMEM],
        out_specs=VMEM,
        scratch_shapes=[pltpu.VMEM((128, 128), jnp.int32), pltpu.VMEM((128 // NCLS, count), jnp.int32)],
        compiler_params=pltpu.CompilerParams(vmem_limit_bytes=16 * MIB),
        cost_estimate=pl.CostEstimate(
            flops=8 * rows * count, bytes_accessed=2 * rows * count, transcendentals=0
        ),
        name="signs",
    )(seeds)


def score_kernel(train_blocks, test_blocks, train_count, test_count, *refs):
    steps = transfer_steps(train_blocks, test_blocks)
    packets = refs[: len(steps) + 3]
    signs = refs[len(steps) + 3 : -5]
    precond_ref, keep_ref, send_ref, train_feat, test_feat = refs[-5:]
    proj_index = lax.axis_index("proj")
    parts, _, part_width = signs[0].shape
    train_rows = train_blocks * train_count
    blocks = {"train": [], "test": []}
    for kind, first, count in (
        ("train", 0, train_count),
        ("test", train_count + 2 * NCLS, test_count),
    ):
        rows = pl.ds(first, count + 2 * NCLS)
        blocks[kind].append((0, [as_float(packet[rows, :]) for packet in packets[:2]]))
    swapped = packets[-1]
    base = 0
    for i, pair in enumerate(steps):
        direct = packets[i + 2]
        for core, (kind, shift) in enumerate(pair):
            size = (train_count if kind == "train" else test_count) + 2 * NCLS
            blocks[kind].append(
                (
                    shift,
                    [
                        jnp.where(
                            proj_index == core,
                            as_float(direct[side, pl.ds(0, size), :]),
                            as_float(swapped[pl.ds(base + (1 - side) * direct.shape[1], size), :]),
                        )
                        for side in range(2)
                    ],
                )
            )
        base += 2 * direct.shape[1]
    gradients = []
    row_weights = []
    for i, (_, pair) in enumerate(blocks["train"] + blocks["test"]):
        count = train_count if i < train_blocks else test_count
        decoded = [decode_packet(packet) for packet in pair]
        values = [value for value, _, _, _ in decoded]
        sizes = [step for _, step, _, _ in decoded]
        logits = decoded[0][2] + decoded[1][2]
        label = decoded[0][3]
        chance = 1.0 / (1.0 + jnp.exp(-logits))
        classes = lax.broadcasted_iota(jnp.int32, (NCLS, 128), 0).astype(jnp.float32)
        target = jnp.where(label == classes, 1.0, 0.0)
        retain = 1.0 - jnp.sum(chance * target, axis=0, keepdims=True)
        rest = [retain, *sizes]
        rest += [jnp.zeros((NCLS - len(rest), 128), jnp.float32)]
        turned = jnp.concatenate([chance - target, *rest], axis=0).T[:count]
        if i < train_blocks:
            row_weights.append(turned[:, NCLS : NCLS + 1])
        pieces = []
        for value_index, value in enumerate(values):
            value = value * turned[:, NCLS + 1 + value_index : NCLS + 2 + value_index]
            for k in range(NCLS):
                pieces.append((value * turned[:, k : k + 1]).astype(jnp.bfloat16))
        gradients.append(jnp.concatenate(pieces, axis=1))
    gradient = jnp.concatenate(gradients, axis=0)
    train_index, test_index = lax.axis_index("train"), lax.axis_index("test")
    for n in range(parts):
        projected = jnp.dot(
            gradient,
            jnp.concatenate([value[n] for value in signs], axis=0),
            preferred_element_type=jnp.float32,
        )
        columns = pl.ds(n * part_width, part_width)
        for i in range(train_blocks):
            part = projected[i * train_count : (i + 1) * train_count]
            train_feat[train_index ^ blocks["train"][i][0], :, columns] = (
                part * row_weights[i]
            ).astype(jnp.bfloat16)
        precond = precond_ref[
            :, pl.ds(pl.multiple_of(proj_index * (parts * part_width) + n * part_width, 128), part_width)
        ]
        for i in range(test_blocks):
            start = train_rows + i * test_count
            test_feat[test_index ^ blocks["test"][i][0], :, columns] = (
                projected[start : start + test_count] * precond
            ).astype(jnp.bfloat16)
    half_blocks = train_blocks // 2
    test = test_feat[...].reshape(test_blocks * test_count, parts * part_width)
    for target, side in ((send_ref, 1 - proj_index), (keep_ref, proj_index)):
        train = train_feat[pl.ds(side * half_blocks, half_blocks)].reshape(
            half_blocks * train_count, parts * part_width
        )
        target[...] = lax.dot_general(
            test, train, (((1,), (1,)), ((), ())), preferred_element_type=jnp.float32
        )


def partial_scores(packets, signs, precond, train_blocks, test_blocks, train_count, test_count):
    parts, _, part_width = signs[0].shape
    rows = sum(value.shape[1] for value in signs)
    out_rows = test_blocks * test_count
    out_cols = train_blocks * train_count
    total_rows = out_rows + out_cols
    return pl.pallas_call(
        functools.partial(score_kernel, train_blocks, test_blocks, train_count, test_count),
        out_shape=(jax.ShapeDtypeStruct((out_rows, out_cols // 2), jnp.float32),) * 2,
        in_specs=[VMEM] * (len(packets) + len(signs) + 1),
        out_specs=(VMEM, VMEM),
        scratch_shapes=[
            pltpu.VMEM((train_blocks, train_count, parts * part_width), jnp.bfloat16),
            pltpu.VMEM((test_blocks, test_count, parts * part_width), jnp.bfloat16),
        ],
        compiler_params=pltpu.CompilerParams(vmem_limit_bytes=40 * MIB),
        cost_estimate=pl.CostEstimate(
            flops=2 * total_rows * rows * parts * part_width,
            bytes_accessed=2 * rows * parts * part_width,
            transcendentals=0,
        ),
        name="partial_scores",
    )(*packets, *signs, precond)


def shards(
    train_windows,
    test_windows,
    train_labels,
    test_labels,
    dilated_weight,
    branch_gain,
    cls_weight,
    sign_seeds,
    precond,
):
    train_count = train_windows.shape[0]
    test_count = test_windows.shape[0]
    train_blocks = lax.axis_size("train")
    test_blocks = lax.axis_size("test")
    count = K // lax.axis_size("proj")
    swap = [(0, 1), (1, 0)]
    seeds = sign_seeds.reshape(-1, 128)
    packet = pool(
        train_windows,
        test_windows,
        dilated_weight,
        branch_gain.reshape(1, -1),
        cls_weight.T,
        train_labels.reshape(1, -1),
        test_labels.reshape(1, -1),
        seeds,
    )
    channels = sign_seeds.shape[0] // NCLS
    halves = (tuple(range(NCLS // 2)), tuple(range(NCLS // 2, NCLS)))
    steps = transfer_steps(train_blocks, test_blocks)
    other_packet = lax.ppermute(packet, "proj", swap)
    signs = [sign_block(seeds, channels, count, halves[0])]
    other_packet, signs[0] = lax.optimization_barrier((other_packet, signs[0]))
    kinds = list(dict.fromkeys((a, b) for (a, _), (b, _) in steps))
    packed = pack(kinds, train_count + 2 * NCLS, test_count + 2 * NCLS, packet, other_packet)
    far = []
    for pair in steps:
        moves = []
        for source in range(train_blocks * test_blocks * 2):
            core = source % 2
            kind, shift = pair[core]
            scale = 2 * test_blocks if kind == "train" else 2
            moves.append((source, source ^ (shift * scale)))
        value = packed[kinds.index((pair[0][0], pair[1][0]))]
        far.append(lax.ppermute(value, ("train", "test", "proj"), moves))
    signs.append(sign_block(seeds, channels, count, halves[1]))
    signs.append(sign_block(other_packet, channels, count, halves[0]))
    *far, signs[1], signs[2] = lax.optimization_barrier((*far, signs[1], signs[2]))
    packets = [packet, other_packet, *far, lax.ppermute(join(far), "proj", swap)]
    signs.append(sign_block(other_packet, channels, count, halves[1]))
    keep, send = partial_scores(
        packets, signs, precond.reshape(1, -1), train_blocks, test_blocks, train_count, test_count
    )
    received = lax.ppermute(send, "proj", swap)
    return (keep + received) * (1.0 / (K * math.sqrt(C)))


def solution(mesh):
    return jax.shard_map(
        shards,
        mesh=mesh,
        in_specs=(
            P(("grp", "test", "train"), None, None),
            P(("grp", "train", "test"), None, None),
            P(("grp", "test", "train")),
            P(("grp", "train", "test")),
            P(None, None, "proj"),
            P("proj"),
            P("proj", None),
            P("proj"),
            P(),
        ),
        out_specs=P(("grp", "train"), ("test", "proj")),
        check_vma=False,
    )
```

```python
import functools
import math

import jax
import jax.numpy as jnp
from jax import lax
from jax.experimental import pallas as pl
from jax.experimental.pallas import tpu as pltpu
from jax.sharding import PartitionSpec as P

C = 512
NCLS = 8
K = 2048
DILATION_STEP = 4
MIX_COLUMN = 668265261
MIX_FIRST = 625341585
MIX_LAST = (1274126177 << 15) & 0xFFFFFFFF
MIX_LAST = MIX_LAST - (1 << 32) if MIX_LAST >= 1 << 31 else MIX_LAST
MIB = 2**20
AHEAD = 2
PART = 64

VMEM = pl.BlockSpec(memory_space=pltpu.VMEM)
HBM = pl.BlockSpec(memory_space=pltpu.HBM)


def write_signs(classes, seeds, sign_ref, turned, column_ref):
    proj_index = lax.axis_index("proj")
    parts, rows, part_width = sign_ref.shape
    count = parts * part_width
    per_chunk = 128 // NCLS
    chunks = rows // (per_chunk * len(classes))
    turned[:, pl.ds(0, chunks)] = seeds.T

    @pl.when(proj_index >= 0)
    def _():
        column_ref[...] = (
            lax.broadcasted_iota(jnp.int32, column_ref.shape, 1) + proj_index * count
        ) * MIX_COLUMN

    for k in classes:
        class_seeds = turned[pl.ds(k, per_chunk, stride=NCLS), :]
        for h in range(chunks):
            mixed = (class_seeds[:, h : h + 1] ^ column_ref[...]) * MIX_FIRST
            mixed = (mixed ^ (mixed >> 13)) * MIX_LAST
            signs = jnp.where(mixed < 0, -1.0, 1.0).astype(jnp.bfloat16)
            at = ((k - classes[0]) * chunks + h) * per_chunk
            for n in range(parts):
                sign_ref[n, pl.ds(at, per_chunk), :] = signs[:, n * part_width : (n + 1) * part_width]


def power_of_two(exponent):
    return jnp.exp(exponent * math.log(2.0))


def encode_packet(packet, at, pooled, logits, labels):
    count = pooled.shape[0]
    largest = jnp.maximum(jnp.max(jnp.abs(pooled), axis=1, keepdims=True), 1e-30)
    exponent = jnp.floor(jnp.log(largest) * (1.0 / math.log(2.0)))
    factor = jnp.ceil(largest * power_of_two(-exponent) * 8192.0)
    step = factor * (power_of_two(exponent) * (1.0 / (8192.0 * 32767.0)))
    steps = jnp.clip(jnp.round(pooled * (1.0 / step)), -32767.0, 32767.0)
    packet[pl.ds(at, count), :] = steps.astype(jnp.int32).astype(jnp.int16)
    lane = lax.broadcasted_iota(jnp.int32, (count, 128), 1)
    turned = jnp.where(lane == 1, factor, jnp.where(lane == 2, exponent, 0.0)).T[:NCLS]
    logit_exponent = jnp.ceil(
        jnp.log(jnp.maximum(jnp.max(jnp.abs(logits), axis=0, keepdims=True), 1e-30)) * (1.0 / math.log(2.0))
    )
    scaled = logits * (power_of_two(-logit_exponent) * 8192.0)
    high = jnp.round(scaled)
    low = jnp.round((scaled - high) * 16384.0)
    row = lax.broadcasted_iota(jnp.int32, (NCLS, count), 0)
    facts = jnp.where(row == 0, labels, jnp.where(row == 3, logit_exponent, turned))
    blank = jnp.zeros((NCLS, PART - count), jnp.float32)
    pieces = [value for part in (high, low, facts) for value in ((part, blank) if count < PART else (part,))]
    pieces.append(jnp.zeros((NCLS, pooled.shape[1] - 3 * PART), jnp.float32))
    return jnp.concatenate(pieces, axis=1).astype(jnp.int32)


def decode_packet(packet):
    count = packet.shape[0] - NCLS
    extra = packet[count:]
    facts = extra[:, 128:]
    step = facts[1:2] * (power_of_two(facts[2:3]) * (1.0 / (8192.0 * 32767.0)))
    high = extra[:, :128]
    logits = (high + pltpu.roll(high, PART, 1) * (1.0 / 16384.0)) * (
        power_of_two(facts[3:4]) * (1.0 / 8192.0)
    )
    return packet[:count], step, logits, facts[0:1]


def as_float(values):
    return values.astype(jnp.int32).astype(jnp.float32)


def pool_kernel(
    block,
    train_hbm,
    test_hbm,
    weight_hbm,
    gain_ref,
    cls_ref,
    train_label_ref,
    test_label_ref,
    seed_ref,
    packet,
    rows,
    weight,
    pooled,
    gain_row,
    cls_rows,
    train_label,
    test_label,
    seeds,
    row_sem,
    weight_sem,
    small_sem,
):
    proj_index = lax.axis_index("proj")
    train_count, length, width = train_hbm.shape
    test_count = test_hbm.shape[0]
    half = weight.shape[2]
    blocks = (train_count + test_count) // block
    small = [
        pltpu.make_async_copy(source, target, small_sem.at[i])
        for i, (source, target) in enumerate(
            (
                (gain_ref, gain_row),
                (cls_ref, cls_rows),
                (train_label_ref, train_label),
                (test_label_ref, test_label),
                (seed_ref, seeds),
            )
        )
    ]
    for copy in small:
        copy.start()
    weight_copy = pltpu.make_async_copy(weight_hbm, weight, weight_sem)
    weight_copy.start()

    def fetch(b):
        source = train_hbm if b < train_count // block else test_hbm
        offset = b * block if b < train_count // block else b * block - train_count
        return pltpu.make_async_copy(
            source.at[pl.ds(offset, block)], rows.at[pl.ds(b * block, block)], row_sem.at[b]
        )

    for b in range(min(AHEAD, blocks)):
        fetch(b).start()
    for copy in small:
        copy.wait()
    weight_copy.wait()
    gain = gain_row[...]
    own_start = pl.multiple_of(proj_index * half, half)

    def one_block(b, carry):
        start = b * block
        for late in range(AHEAD, blocks):

            @pl.when(b == late - AHEAD)
            def _():
                fetch(late).start()

        pltpu.make_async_copy(
            test_hbm.at[pl.ds(0, block)], rows.at[pl.ds(start, block)], row_sem.at[b]
        ).wait()
        x = rows[pl.ds(start, block)]
        zeros = jnp.zeros((block, DILATION_STEP, width), x.dtype)
        before = jnp.concatenate([zeros, x[:, : length - DILATION_STEP]], axis=1)
        after = jnp.concatenate([x[:, DILATION_STEP:], zeros], axis=1)
        taps = jnp.concatenate([before, x, after], axis=2).reshape(block * length, 3 * width)
        conv = jnp.dot(
            taps, weight[...].reshape(3 * width, half), preferred_element_type=jnp.float32
        ).reshape(block, length, half)
        own = rows[pl.ds(start, block), :, pl.ds(own_start, half)].astype(jnp.float32)
        total = jnp.sum(own, axis=1) + gain * jnp.sum(jnp.maximum(conv, 0.0), axis=1)
        pooled[pl.ds(pl.multiple_of(start, block), block), :] = total * (1.0 / length)
        return carry

    lax.fori_loop(0, blocks, one_block, 0)
    extra = []
    for label_ref, start, count in ((train_label, 0, train_count), (test_label, train_count, test_count)):
        own = pooled[pl.ds(start, count), :]
        logits = lax.dot_general(
            cls_rows[...],
            own,
            (((1,), (1,)), ((), ())),
            precision=lax.Precision.HIGHEST,
            preferred_element_type=jnp.float32,
        )
        labels = jnp.broadcast_to(label_ref[...].astype(jnp.float32), (NCLS, count))
        extra.append(encode_packet(packet, start, own, logits, labels))
    at = train_count + test_count
    packet[pl.ds(at, 2 * NCLS), :] = jnp.concatenate(extra, axis=0).astype(jnp.int16)
    at += 2 * NCLS
    packet[pl.ds(at, seeds.shape[0]), pl.ds(0, 128)] = (seeds[...] >> 15).astype(jnp.int16)
    packet[pl.ds(at, seeds.shape[0]), pl.ds(128, 128)] = (seeds[...] & 32767).astype(jnp.int16)


def pool(train_windows, test_windows, weight, gain, cls_t, train_labels, test_labels, seeds):
    block = 16
    train_count, length, width = train_windows.shape
    test_count = test_windows.shape[0]
    half = weight.shape[2]
    total = train_count + test_count
    return pl.pallas_call(
        functools.partial(pool_kernel, block),
        out_shape=jax.ShapeDtypeStruct((total + 2 * NCLS + seeds.shape[0], half), jnp.int16),
        in_specs=[HBM] * 8,
        out_specs=VMEM,
        scratch_shapes=[
            pltpu.VMEM((total, length, width), jnp.bfloat16),
            pltpu.VMEM(weight.shape, jnp.bfloat16),
            pltpu.VMEM((total, half), jnp.float32),
            pltpu.VMEM(gain.shape, jnp.float32),
            pltpu.VMEM(cls_t.shape, jnp.float32),
            pltpu.VMEM(train_labels.shape, jnp.int32),
            pltpu.VMEM(test_labels.shape, jnp.int32),
            pltpu.VMEM(seeds.shape, jnp.int32),
            pltpu.SemaphoreType.DMA((total // block,)),
            pltpu.SemaphoreType.DMA,
            pltpu.SemaphoreType.DMA((5,)),
        ],
        compiler_params=pltpu.CompilerParams(vmem_limit_bytes=24 * MIB),
        name="pool",
    )(
        *(
            pltpu.with_memory_space_constraint(value, pltpu.HBM)
            for value in (train_windows, test_windows, weight, gain, cls_t, train_labels, test_labels, seeds)
        )
    )


def transfer_steps(train_blocks, test_blocks):
    shifts = [("train", d) for d in reversed(range(1, train_blocks))]
    shifts += [("test", d) for d in range(1, test_blocks)]
    return [(shifts[i + 1], shifts[i]) for i in range(0, len(shifts), 2)]


def pack_kernel(kinds, train_count, test_count, mine, theirs, *outs):
    proj_index = lax.axis_index("proj")
    for pair, out in zip(kinds, outs):
        for core, kind in enumerate(pair):

            @pl.when(proj_index == core)
            def _():
                start, count = (0, train_count) if kind == "train" else (train_count, test_count)
                extra = train_count + test_count + (0 if kind == "train" else NCLS)
                for side, packet in enumerate((mine, theirs)):
                    out[side, pl.ds(0, count), :] = packet[pl.ds(start, count), :]
                    out[side, pl.ds(count, NCLS), :] = packet[pl.ds(extra, NCLS), :]


def pack(kinds, train_count, test_count, mine, theirs):
    width = mine.shape[1]
    rows = [(train_count if "train" in pair else test_count) + NCLS for pair in kinds]
    return pl.pallas_call(
        functools.partial(pack_kernel, kinds, train_count, test_count),
        out_shape=tuple(jax.ShapeDtypeStruct((2, count, width), jnp.int16) for count in rows),
        in_specs=[VMEM, VMEM],
        out_specs=(VMEM,) * len(kinds),
        compiler_params=pltpu.CompilerParams(vmem_limit_bytes=8 * MIB),
        name="pack",
    )(mine, theirs)


def join_kernel(*refs):
    *values, out = refs
    at = 0
    for value in values:
        for side in range(value.shape[0]):
            out[pl.ds(at, value.shape[1]), :] = value[side]
            at += value.shape[1]


def join(values):
    rows = sum(value.shape[0] * value.shape[1] for value in values)
    return pl.pallas_call(
        join_kernel,
        out_shape=jax.ShapeDtypeStruct((rows, values[0].shape[2]), values[0].dtype),
        in_specs=[VMEM] * len(values),
        out_specs=VMEM,
        compiler_params=pltpu.CompilerParams(vmem_limit_bytes=8 * MIB),
        name="join",
    )(*values)


def sign_kernel(packed, classes, seed_ref, sign_ref, turned, column_ref):
    if packed:
        chunks = sign_ref.shape[1] // ((128 // NCLS) * len(classes))
        first = seed_ref.shape[0] - chunks
        high = seed_ref[pl.ds(first, chunks), pl.ds(0, 128)].astype(jnp.int32)
        seeds = high * 32768 + seed_ref[pl.ds(first, chunks), pl.ds(128, 128)].astype(jnp.int32)
    else:
        seeds = seed_ref[...]
    write_signs(classes, seeds, sign_ref, turned, column_ref)


def sign_block(seeds, channels, count, classes):
    rows = channels * len(classes)
    parts = count // 256
    return pl.pallas_call(
        functools.partial(sign_kernel, seeds.dtype == jnp.int16, classes),
        out_shape=jax.ShapeDtypeStruct((parts, rows, 256), jnp.bfloat16),
        in_specs=[VMEM],
        out_specs=VMEM,
        scratch_shapes=[pltpu.VMEM((128, 128), jnp.int32), pltpu.VMEM((128 // NCLS, count), jnp.int32)],
        compiler_params=pltpu.CompilerParams(vmem_limit_bytes=16 * MIB),
        cost_estimate=pl.CostEstimate(
            flops=8 * rows * count, bytes_accessed=2 * rows * count, transcendentals=0
        ),
        name="signs",
    )(seeds)


def score_kernel(train_blocks, test_blocks, train_count, test_count, *refs):
    steps = transfer_steps(train_blocks, test_blocks)
    packets = refs[: len(steps) + 3]
    signs = refs[len(steps) + 3 : -5]
    precond_ref, keep_ref, send_ref, train_feat, test_feat = refs[-5:]
    proj_index = lax.axis_index("proj")
    parts, _, part_width = signs[0].shape
    train_rows = train_blocks * train_count
    blocks = {"train": [], "test": []}
    for kind, first, count, extra in (
        ("train", 0, train_count, train_count + test_count),
        ("test", train_count, test_count, train_count + test_count + NCLS),
    ):
        own = [
            as_float(jnp.concatenate([packet[pl.ds(first, count), :], packet[pl.ds(extra, NCLS), :]], axis=0))
            for packet in packets[:2]
        ]
        blocks[kind].append((0, own))
    swapped = packets[-1]
    base = 0
    for i, pair in enumerate(steps):
        direct = packets[i + 2]
        for core, (kind, shift) in enumerate(pair):
            size = (train_count if kind == "train" else test_count) + NCLS
            blocks[kind].append(
                (
                    shift,
                    [
                        jnp.where(
                            proj_index == core,
                            as_float(direct[side, pl.ds(0, size), :]),
                            as_float(swapped[pl.ds(base + (1 - side) * direct.shape[1], size), :]),
                        )
                        for side in range(2)
                    ],
                )
            )
        base += 2 * direct.shape[1]
    gradients = []
    row_weights = []
    for i, (_, pair) in enumerate(blocks["train"] + blocks["test"]):
        count = train_count if i < train_blocks else test_count
        decoded = [decode_packet(packet) for packet in pair]
        values = [value for value, _, _, _ in decoded]
        sizes = [step for _, step, _, _ in decoded]
        logits = decoded[0][2] + decoded[1][2]
        label = decoded[0][3]
        chance = 1.0 / (1.0 + jnp.exp(-logits))
        classes = lax.broadcasted_iota(jnp.int32, (NCLS, 128), 0).astype(jnp.float32)
        target = jnp.where(label == classes, 1.0, 0.0)
        retain = 1.0 - jnp.sum(chance * target, axis=0, keepdims=True)
        rest = [retain, *sizes]
        rest += [jnp.zeros((NCLS - len(rest), 128), jnp.float32)]
        turned = jnp.concatenate([chance - target, *rest], axis=0).T[:count]
        if i < train_blocks:
            row_weights.append(turned[:, NCLS : NCLS + 1])
        pieces = []
        for value_index, value in enumerate(values):
            value = value * turned[:, NCLS + 1 + value_index : NCLS + 2 + value_index]
            for k in range(NCLS):
                pieces.append((value * turned[:, k : k + 1]).astype(jnp.bfloat16))
        gradients.append(jnp.concatenate(pieces, axis=1))
    gradient = jnp.concatenate(gradients, axis=0)
    train_index, test_index = lax.axis_index("train"), lax.axis_index("test")
    for n in range(parts):
        projected = jnp.dot(
            gradient,
            jnp.concatenate([value[n] for value in signs], axis=0),
            preferred_element_type=jnp.float32,
        )
        columns = pl.ds(n * part_width, part_width)
        for i in range(train_blocks):
            part = projected[i * train_count : (i + 1) * train_count]
            train_feat[train_index ^ blocks["train"][i][0], :, columns] = (
                part * row_weights[i]
            ).astype(jnp.bfloat16)
        precond = precond_ref[
            :, pl.ds(pl.multiple_of(proj_index * (parts * part_width) + n * part_width, 128), part_width)
        ]
        for i in range(test_blocks):
            start = train_rows + i * test_count
            test_feat[test_index ^ blocks["test"][i][0], :, columns] = (
                projected[start : start + test_count] * precond
            ).astype(jnp.bfloat16)
    half_blocks = train_blocks // 2
    test = test_feat[...].reshape(test_blocks * test_count, parts * part_width)
    for target, side in ((send_ref, 1 - proj_index), (keep_ref, proj_index)):
        train = train_feat[pl.ds(side * half_blocks, half_blocks)].reshape(
            half_blocks * train_count, parts * part_width
        )
        target[...] = lax.dot_general(
            test, train, (((1,), (1,)), ((), ())), preferred_element_type=jnp.float32
        )


def partial_scores(packets, signs, precond, train_blocks, test_blocks, train_count, test_count):
    parts, _, part_width = signs[0].shape
    rows = sum(value.shape[1] for value in signs)
    out_rows = test_blocks * test_count
    out_cols = train_blocks * train_count
    total_rows = out_rows + out_cols
    return pl.pallas_call(
        functools.partial(score_kernel, train_blocks, test_blocks, train_count, test_count),
        out_shape=(jax.ShapeDtypeStruct((out_rows, out_cols // 2), jnp.float32),) * 2,
        in_specs=[VMEM] * (len(packets) + len(signs) + 1),
        out_specs=(VMEM, VMEM),
        scratch_shapes=[
            pltpu.VMEM((train_blocks, train_count, parts * part_width), jnp.bfloat16),
            pltpu.VMEM((test_blocks, test_count, parts * part_width), jnp.bfloat16),
        ],
        compiler_params=pltpu.CompilerParams(vmem_limit_bytes=40 * MIB),
        cost_estimate=pl.CostEstimate(
            flops=2 * total_rows * rows * parts * part_width,
            bytes_accessed=2 * rows * parts * part_width,
            transcendentals=0,
        ),
        name="partial_scores",
    )(*packets, *signs, precond)


def shards(
    train_windows,
    test_windows,
    train_labels,
    test_labels,
    dilated_weight,
    branch_gain,
    cls_weight,
    sign_seeds,
    precond,
):
    train_count = train_windows.shape[0]
    test_count = test_windows.shape[0]
    train_blocks = lax.axis_size("train")
    test_blocks = lax.axis_size("test")
    count = K // lax.axis_size("proj")
    swap = [(0, 1), (1, 0)]
    seeds = sign_seeds.reshape(-1, 128)
    packet = pool(
        train_windows,
        test_windows,
        dilated_weight,
        branch_gain.reshape(1, -1),
        cls_weight.T,
        train_labels.reshape(1, -1),
        test_labels.reshape(1, -1),
        seeds,
    )
    channels = sign_seeds.shape[0] // NCLS
    halves = (tuple(range(NCLS // 2)), tuple(range(NCLS // 2, NCLS)))
    steps = transfer_steps(train_blocks, test_blocks)
    other_packet = lax.ppermute(packet, "proj", swap)
    signs = [sign_block(seeds, channels, count, halves[0])]
    other_packet, signs[0] = lax.optimization_barrier((other_packet, signs[0]))
    kinds = list(dict.fromkeys((a, b) for (a, _), (b, _) in steps))
    packed = pack(kinds, train_count, test_count, packet, other_packet)
    far = []
    for pair in steps:
        moves = []
        for source in range(train_blocks * test_blocks * 2):
            core = source % 2
            kind, shift = pair[core]
            scale = 2 * test_blocks if kind == "train" else 2
            moves.append((source, source ^ (shift * scale)))
        value = packed[kinds.index((pair[0][0], pair[1][0]))]
        far.append(lax.ppermute(value, ("train", "test", "proj"), moves))
    signs.append(sign_block(seeds, channels, count, halves[1]))
    signs.append(sign_block(other_packet, channels, count, halves[0]))
    *far, signs[1], signs[2] = lax.optimization_barrier((*far, signs[1], signs[2]))
    packets = [packet, other_packet, *far, lax.ppermute(join(far), "proj", swap)]
    signs.append(sign_block(other_packet, channels, count, halves[1]))
    keep, send = partial_scores(
        packets, signs, precond.reshape(1, -1), train_blocks, test_blocks, train_count, test_count
    )
    received = lax.ppermute(send, "proj", swap)
    return (keep + received) * (1.0 / (K * math.sqrt(C)))


def solution(mesh):
    return jax.shard_map(
        shards,
        mesh=mesh,
        in_specs=(
            P(("grp", "test", "train"), None, None),
            P(("grp", "train", "test"), None, None),
            P(("grp", "test", "train")),
            P(("grp", "train", "test")),
            P(None, None, "proj"),
            P("proj"),
            P("proj", None),
            P("proj"),
            P(),
        ),
        out_specs=P(("grp", "train"), ("test", "proj")),
        check_vma=False,
    )
```

```python
import functools
import math

import jax
import jax.numpy as jnp
from jax import lax
from jax.experimental import pallas as pl
from jax.experimental.pallas import tpu as pltpu
from jax.sharding import PartitionSpec as P

C = 512
NCLS = 8
K = 2048
DILATION_STEP = 4
MIX_COLUMN = 668265261
MIX_FIRST = 625341585
MIX_LAST = (1274126177 << 15) & 0xFFFFFFFF
MIX_LAST = MIX_LAST - (1 << 32) if MIX_LAST >= 1 << 31 else MIX_LAST
MIB = 2**20
AHEAD = 2
PART = 64

VMEM = pl.BlockSpec(memory_space=pltpu.VMEM)
HBM = pl.BlockSpec(memory_space=pltpu.HBM)


def write_signs(classes, seeds, sign_ref, turned, column_ref):
    proj_index = lax.axis_index("proj")
    parts, rows, part_width = sign_ref.shape
    count = parts * part_width
    per_chunk = 128 // NCLS
    chunks = rows // (per_chunk * len(classes))
    turned[:, pl.ds(0, chunks)] = seeds.T

    @pl.when(proj_index >= 0)
    def _():
        column_ref[...] = (
            lax.broadcasted_iota(jnp.int32, column_ref.shape, 1) + proj_index * count
        ) * MIX_COLUMN

    for k in classes:
        class_seeds = turned[pl.ds(k, per_chunk, stride=NCLS), :]
        for h in range(chunks):
            mixed = (class_seeds[:, h : h + 1] ^ column_ref[...]) * MIX_FIRST
            mixed = (mixed ^ (mixed >> 13)) * MIX_LAST
            signs = jnp.where(mixed < 0, -1.0, 1.0).astype(jnp.bfloat16)
            at = ((k - classes[0]) * chunks + h) * per_chunk
            for n in range(parts):
                sign_ref[n, pl.ds(at, per_chunk), :] = signs[:, n * part_width : (n + 1) * part_width]


def power_of_two(exponent):
    return jnp.exp(exponent * math.log(2.0))


def encode_packet(packet, at, pooled, logits, labels):
    count = pooled.shape[0]
    largest = jnp.maximum(jnp.max(jnp.abs(pooled), axis=1, keepdims=True), 1e-30)
    exponent = jnp.floor(jnp.log(largest) * (1.0 / math.log(2.0)))
    factor = jnp.ceil(largest * power_of_two(-exponent) * 8192.0)
    step = factor * (power_of_two(exponent) * (1.0 / (8192.0 * 32767.0)))
    steps = jnp.clip(jnp.round(pooled * (1.0 / step)), -32767.0, 32767.0)
    packet[pl.ds(at, count), :] = steps.astype(jnp.int32).astype(jnp.int16)
    lane = lax.broadcasted_iota(jnp.int32, (count, 128), 1)
    turned = jnp.where(lane == 1, factor, jnp.where(lane == 2, exponent, 0.0)).T[:NCLS]
    logit_exponent = jnp.ceil(
        jnp.log(jnp.maximum(jnp.max(jnp.abs(logits), axis=0, keepdims=True), 1e-30)) * (1.0 / math.log(2.0))
    )
    scaled = logits * (power_of_two(-logit_exponent) * 8192.0)
    high = jnp.round(scaled)
    low = jnp.round((scaled - high) * 16384.0)
    row = lax.broadcasted_iota(jnp.int32, (NCLS, count), 0)
    facts = jnp.where(row == 0, labels, jnp.where(row == 3, logit_exponent, turned))
    blank = jnp.zeros((NCLS, PART - count), jnp.float32)
    pieces = [value for part in (high, low, facts) for value in ((part, blank) if count < PART else (part,))]
    pieces.append(jnp.zeros((NCLS, pooled.shape[1] - 3 * PART), jnp.float32))
    return jnp.concatenate(pieces, axis=1).astype(jnp.int32)


def decode_packet(packet):
    count = packet.shape[0] - NCLS
    extra = packet[count:]
    facts = extra[:, 128:]
    step = facts[1:2] * (power_of_two(facts[2:3]) * (1.0 / (8192.0 * 32767.0)))
    high = extra[:, :128]
    logits = (high + pltpu.roll(high, PART, 1) * (1.0 / 16384.0)) * (
        power_of_two(facts[3:4]) * (1.0 / 8192.0)
    )
    return packet[:count], step, logits, facts[0:1]


def as_float(values):
    return values.astype(jnp.int32).astype(jnp.float32)


def pool_kernel(
    block,
    train_hbm,
    test_hbm,
    weight_hbm,
    gain_ref,
    cls_ref,
    train_label_ref,
    test_label_ref,
    seed_ref,
    packet,
    rows,
    weight,
    pooled,
    gain_row,
    cls_rows,
    train_label,
    test_label,
    seeds,
    row_sem,
    weight_sem,
    small_sem,
):
    proj_index = lax.axis_index("proj")
    train_count, length, width = train_hbm.shape
    test_count = test_hbm.shape[0]
    half = weight.shape[2]
    blocks = (train_count + test_count) // block
    small = [
        pltpu.make_async_copy(source, target, small_sem.at[i])
        for i, (source, target) in enumerate(
            (
                (gain_ref, gain_row),
                (cls_ref, cls_rows),
                (train_label_ref, train_label),
                (test_label_ref, test_label),
                (seed_ref, seeds),
            )
        )
    ]
    for copy in small:
        copy.start()
    weight_copy = pltpu.make_async_copy(weight_hbm, weight, weight_sem)
    weight_copy.start()

    def fetch(b):
        source = train_hbm if b < train_count // block else test_hbm
        offset = b * block if b < train_count // block else b * block - train_count
        return pltpu.make_async_copy(
            source.at[pl.ds(offset, block)], rows.at[pl.ds(b * block, block)], row_sem.at[b]
        )

    for b in range(min(AHEAD, blocks)):
        fetch(b).start()
    for copy in small:
        copy.wait()
    weight_copy.wait()
    gain = gain_row[...]
    own_start = pl.multiple_of(proj_index * half, half)

    def one_block(b, carry):
        start = b * block
        for late in range(AHEAD, blocks):

            @pl.when(b == late - AHEAD)
            def _():
                fetch(late).start()

        pltpu.make_async_copy(
            test_hbm.at[pl.ds(0, block)], rows.at[pl.ds(start, block)], row_sem.at[b]
        ).wait()
        x = rows[pl.ds(start, block)]
        zeros = jnp.zeros((block, DILATION_STEP, width), x.dtype)
        before = jnp.concatenate([zeros, x[:, : length - DILATION_STEP]], axis=1)
        after = jnp.concatenate([x[:, DILATION_STEP:], zeros], axis=1)
        taps = jnp.concatenate([before, x, after], axis=2).reshape(block * length, 3 * width)
        conv = jnp.dot(
            taps, weight[...].reshape(3 * width, half), preferred_element_type=jnp.float32
        ).reshape(block, length, half)
        own = rows[pl.ds(start, block), :, pl.ds(own_start, half)].astype(jnp.float32)
        total = jnp.sum(own, axis=1) + gain * jnp.sum(jnp.maximum(conv, 0.0), axis=1)
        pooled[pl.ds(pl.multiple_of(start, block), block), :] = total * (1.0 / length)
        return carry

    lax.fori_loop(0, blocks, one_block, 0)
    extra = []
    for label_ref, start, count in ((train_label, 0, train_count), (test_label, train_count, test_count)):
        own = pooled[pl.ds(start, count), :]
        logits = lax.dot_general(
            cls_rows[...],
            own,
            (((1,), (1,)), ((), ())),
            precision=lax.Precision.HIGHEST,
            preferred_element_type=jnp.float32,
        )
        labels = jnp.broadcast_to(label_ref[...].astype(jnp.float32), (NCLS, count))
        extra.append(encode_packet(packet, start, own, logits, labels))
    at = train_count + test_count
    packet[pl.ds(at, 2 * NCLS), :] = jnp.concatenate(extra, axis=0).astype(jnp.int16)
    at += 2 * NCLS
    packet[pl.ds(at, seeds.shape[0]), pl.ds(0, 128)] = (seeds[...] >> 15).astype(jnp.int16)
    packet[pl.ds(at, seeds.shape[0]), pl.ds(128, 128)] = (seeds[...] & 32767).astype(jnp.int16)


def pool(train_windows, test_windows, weight, gain, cls_t, train_labels, test_labels, seeds):
    block = 16
    train_count, length, width = train_windows.shape
    test_count = test_windows.shape[0]
    half = weight.shape[2]
    total = train_count + test_count
    return pl.pallas_call(
        functools.partial(pool_kernel, block),
        out_shape=jax.ShapeDtypeStruct((total + 2 * NCLS + seeds.shape[0], half), jnp.int16),
        in_specs=[HBM] * 8,
        out_specs=VMEM,
        scratch_shapes=[
            pltpu.VMEM((total, length, width), jnp.bfloat16),
            pltpu.VMEM(weight.shape, jnp.bfloat16),
            pltpu.VMEM((total, half), jnp.float32),
            pltpu.VMEM(gain.shape, jnp.float32),
            pltpu.VMEM(cls_t.shape, jnp.float32),
            pltpu.VMEM(train_labels.shape, jnp.int32),
            pltpu.VMEM(test_labels.shape, jnp.int32),
            pltpu.VMEM(seeds.shape, jnp.int32),
            pltpu.SemaphoreType.DMA((total // block,)),
            pltpu.SemaphoreType.DMA,
            pltpu.SemaphoreType.DMA((5,)),
        ],
        compiler_params=pltpu.CompilerParams(vmem_limit_bytes=24 * MIB),
        name="pool",
    )(
        *(
            pltpu.with_memory_space_constraint(value, pltpu.HBM)
            for value in (train_windows, test_windows, weight, gain, cls_t, train_labels, test_labels, seeds)
        )
    )


def transfer_steps(train_blocks, test_blocks):
    shifts = [("train", d) for d in reversed(range(1, train_blocks))]
    shifts += [("test", d) for d in range(1, test_blocks)]
    return [(shifts[i + 1], shifts[i]) for i in range(0, len(shifts), 2)]


def pack_kernel(kinds, train_count, test_count, mine, theirs, *outs):
    proj_index = lax.axis_index("proj")
    for pair, out in zip(kinds, outs):
        for core, kind in enumerate(pair):

            @pl.when(proj_index == core)
            def _():
                start, count = (0, train_count) if kind == "train" else (train_count, test_count)
                extra = train_count + test_count + (0 if kind == "train" else NCLS)
                for side, packet in enumerate((mine, theirs)):
                    out[side, pl.ds(0, count), :] = packet[pl.ds(start, count), :]
                    out[side, pl.ds(count, NCLS), :] = packet[pl.ds(extra, NCLS), :]


def pack(kinds, train_count, test_count, mine, theirs):
    width = mine.shape[1]
    rows = [(train_count if "train" in pair else test_count) + NCLS for pair in kinds]
    return pl.pallas_call(
        functools.partial(pack_kernel, kinds, train_count, test_count),
        out_shape=tuple(jax.ShapeDtypeStruct((2, count, width), jnp.int16) for count in rows),
        in_specs=[VMEM, VMEM],
        out_specs=(VMEM,) * len(kinds),
        compiler_params=pltpu.CompilerParams(vmem_limit_bytes=8 * MIB),
        name="pack",
    )(mine, theirs)


def join_kernel(*refs):
    *values, out = refs
    at = 0
    for value in values:
        for side in range(value.shape[0]):
            out[pl.ds(at, value.shape[1]), :] = value[side]
            at += value.shape[1]


def join(values):
    rows = sum(value.shape[0] * value.shape[1] for value in values)
    return pl.pallas_call(
        join_kernel,
        out_shape=jax.ShapeDtypeStruct((rows, values[0].shape[2]), values[0].dtype),
        in_specs=[VMEM] * len(values),
        out_specs=VMEM,
        compiler_params=pltpu.CompilerParams(vmem_limit_bytes=8 * MIB),
        name="join",
    )(*values)


def sign_kernel(packed, classes, seed_ref, sign_ref, turned, column_ref):
    if packed:
        chunks = sign_ref.shape[1] // ((128 // NCLS) * len(classes))
        first = seed_ref.shape[0] - chunks
        high = seed_ref[pl.ds(first, chunks), pl.ds(0, 128)].astype(jnp.int32)
        seeds = high * 32768 + seed_ref[pl.ds(first, chunks), pl.ds(128, 128)].astype(jnp.int32)
    else:
        seeds = seed_ref[...]
    write_signs(classes, seeds, sign_ref, turned, column_ref)


def sign_block(seeds, channels, count, classes):
    rows = channels * len(classes)
    parts = count // 256
    return pl.pallas_call(
        functools.partial(sign_kernel, seeds.dtype == jnp.int16, classes),
        out_shape=jax.ShapeDtypeStruct((parts, rows, 256), jnp.bfloat16),
        in_specs=[VMEM],
        out_specs=VMEM,
        scratch_shapes=[pltpu.VMEM((128, 128), jnp.int32), pltpu.VMEM((128 // NCLS, count), jnp.int32)],
        compiler_params=pltpu.CompilerParams(vmem_limit_bytes=16 * MIB),
        cost_estimate=pl.CostEstimate(
            flops=8 * rows * count, bytes_accessed=2 * rows * count, transcendentals=0
        ),
        name="signs",
    )(seeds)


def score_kernel(train_blocks, test_blocks, train_count, test_count, *refs):
    steps = transfer_steps(train_blocks, test_blocks)
    packets = refs[: len(steps) + 3]
    signs = refs[len(steps) + 3 : -5]
    precond_ref, keep_ref, send_ref, train_feat, test_feat = refs[-5:]
    proj_index = lax.axis_index("proj")
    parts, _, part_width = signs[0].shape
    train_rows = train_blocks * train_count
    blocks = {"train": [], "test": []}
    for kind, first, count, extra in (
        ("train", 0, train_count, train_count + test_count),
        ("test", train_count, test_count, train_count + test_count + NCLS),
    ):
        own = [
            as_float(jnp.concatenate([packet[pl.ds(first, count), :], packet[pl.ds(extra, NCLS), :]], axis=0))
            for packet in packets[:2]
        ]
        blocks[kind].append((0, own))
    swapped = packets[-1]
    base = 0
    for i, pair in enumerate(steps):
        direct = packets[i + 2]
        for core, (kind, shift) in enumerate(pair):
            size = (train_count if kind == "train" else test_count) + NCLS
            blocks[kind].append(
                (
                    shift,
                    [
                        jnp.where(
                            proj_index == core,
                            as_float(direct[side, pl.ds(0, size), :]),
                            as_float(swapped[pl.ds(base + (1 - side) * direct.shape[1], size), :]),
                        )
                        for side in range(2)
                    ],
                )
            )
        base += 2 * direct.shape[1]
    gradients = []
    row_weights = []
    for i, (_, pair) in enumerate(blocks["train"] + blocks["test"]):
        count = train_count if i < train_blocks else test_count
        decoded = [decode_packet(packet) for packet in pair]
        values = [value for value, _, _, _ in decoded]
        sizes = [step for _, step, _, _ in decoded]
        logits = decoded[0][2] + decoded[1][2]
        label = decoded[0][3]
        chance = 1.0 / (1.0 + jnp.exp(-logits))
        classes = lax.broadcasted_iota(jnp.int32, (NCLS, 128), 0).astype(jnp.float32)
        target = jnp.where(label == classes, 1.0, 0.0)
        retain = 1.0 - jnp.sum(chance * target, axis=0, keepdims=True)
        rest = [retain, *sizes]
        rest += [jnp.zeros((NCLS - len(rest), 128), jnp.float32)]
        turned = jnp.concatenate([chance - target, *rest], axis=0).T[:count]
        if i < train_blocks:
            row_weights.append(turned[:, NCLS : NCLS + 1])
        pieces = []
        for value_index, value in enumerate(values):
            value = value * turned[:, NCLS + 1 + value_index : NCLS + 2 + value_index]
            for k in range(NCLS):
                pieces.append((value * turned[:, k : k + 1]).astype(jnp.bfloat16))
        gradients.append(jnp.concatenate(pieces, axis=1))
    gradient = jnp.concatenate(gradients, axis=0)
    train_index, test_index = lax.axis_index("train"), lax.axis_index("test")
    for n in range(parts):
        projected = jnp.dot(
            gradient,
            jnp.concatenate([value[n] for value in signs], axis=0),
            preferred_element_type=jnp.float32,
        )
        columns = pl.ds(n * part_width, part_width)
        for i in range(train_blocks):
            part = projected[i * train_count : (i + 1) * train_count]
            train_feat[train_index ^ blocks["train"][i][0], :, columns] = (
                part * row_weights[i]
            ).astype(jnp.bfloat16)
        precond = precond_ref[
            :, pl.ds(pl.multiple_of(proj_index * (parts * part_width) + n * part_width, 128), part_width)
        ]
        for i in range(test_blocks):
            start = train_rows + i * test_count
            test_feat[test_index ^ blocks["test"][i][0], :, columns] = (
                projected[start : start + test_count] * precond
            ).astype(jnp.bfloat16)
    half_blocks = train_blocks // 2
    test = test_feat[...].reshape(test_blocks * test_count, parts * part_width)
    for target, side in ((send_ref, 1 - proj_index), (keep_ref, proj_index)):
        train = train_feat[pl.ds(side * half_blocks, half_blocks)].reshape(
            half_blocks * train_count, parts * part_width
        )
        target[...] = lax.dot_general(
            test, train, (((1,), (1,)), ((), ())), preferred_element_type=jnp.float32
        )


def partial_scores(packets, signs, precond, train_blocks, test_blocks, train_count, test_count):
    parts, _, part_width = signs[0].shape
    rows = sum(value.shape[1] for value in signs)
    out_rows = test_blocks * test_count
    out_cols = train_blocks * train_count
    total_rows = out_rows + out_cols
    return pl.pallas_call(
        functools.partial(score_kernel, train_blocks, test_blocks, train_count, test_count),
        out_shape=(jax.ShapeDtypeStruct((out_rows, out_cols // 2), jnp.float32),) * 2,
        in_specs=[VMEM] * (len(packets) + len(signs) + 1),
        out_specs=(VMEM, VMEM),
        scratch_shapes=[
            pltpu.VMEM((train_blocks, train_count, parts * part_width), jnp.bfloat16),
            pltpu.VMEM((test_blocks, test_count, parts * part_width), jnp.bfloat16),
        ],
        compiler_params=pltpu.CompilerParams(vmem_limit_bytes=40 * MIB),
        cost_estimate=pl.CostEstimate(
            flops=2 * total_rows * rows * parts * part_width,
            bytes_accessed=2 * rows * parts * part_width,
            transcendentals=0,
        ),
        name="partial_scores",
    )(*packets, *signs, precond)


def shards(
    train_windows,
    test_windows,
    train_labels,
    test_labels,
    dilated_weight,
    branch_gain,
    cls_weight,
    sign_seeds,
    precond,
):
    train_count = train_windows.shape[0]
    test_count = test_windows.shape[0]
    train_blocks = lax.axis_size("train")
    test_blocks = lax.axis_size("test")
    count = K // lax.axis_size("proj")
    swap = [(0, 1), (1, 0)]
    seeds = sign_seeds.reshape(-1, 128)
    packet = pool(
        train_windows,
        test_windows,
        dilated_weight,
        branch_gain.reshape(1, -1),
        cls_weight.T,
        train_labels.reshape(1, -1),
        test_labels.reshape(1, -1),
        seeds,
    )
    channels = sign_seeds.shape[0] // NCLS
    halves = (tuple(range(NCLS // 2)), tuple(range(NCLS // 2, NCLS)))
    steps = transfer_steps(train_blocks, test_blocks)
    other_packet = lax.ppermute(packet, "proj", swap)
    signs = [sign_block(seeds, channels, count, tuple(range(3)))]
    other_packet, signs[0] = lax.optimization_barrier((other_packet, signs[0]))
    kinds = list(dict.fromkeys((a, b) for (a, _), (b, _) in steps))
    packed = pack(kinds, train_count, test_count, packet, other_packet)
    far = []
    for pair in steps:
        moves = []
        for source in range(train_blocks * test_blocks * 2):
            core = source % 2
            kind, shift = pair[core]
            scale = 2 * test_blocks if kind == "train" else 2
            moves.append((source, source ^ (shift * scale)))
        value = packed[kinds.index((pair[0][0], pair[1][0]))]
        far.append(lax.ppermute(value, ("train", "test", "proj"), moves))
    signs.append(sign_block(seeds, channels, count, tuple(range(3, NCLS))))
    signs.append(sign_block(other_packet, channels, count, halves[0]))
    *far, signs[1], signs[2] = lax.optimization_barrier((*far, signs[1], signs[2]))
    packets = [packet, other_packet, *far, lax.ppermute(join(far), "proj", swap)]
    signs.append(sign_block(other_packet, channels, count, halves[1]))
    keep, send = partial_scores(
        packets, signs, precond.reshape(1, -1), train_blocks, test_blocks, train_count, test_count
    )
    received = lax.ppermute(send, "proj", swap)
    return (keep + received) * (1.0 / (K * math.sqrt(C)))


def solution(mesh):
    return jax.shard_map(
        shards,
        mesh=mesh,
        in_specs=(
            P(("grp", "test", "train"), None, None),
            P(("grp", "train", "test"), None, None),
            P(("grp", "test", "train")),
            P(("grp", "train", "test")),
            P(None, None, "proj"),
            P("proj"),
            P("proj", None),
            P("proj"),
            P(),
        ),
        out_specs=P(("grp", "train"), ("test", "proj")),
        check_vma=False,
    )
```
